32 devices in a mesh: terms: 8 (over y, x, core), rows: 4 (over z).
Axes of the slice: x: 2, y: 2, z: 4, core: 2. Of those that a mesh axis runs over, the one named last changes fastest.
Arguments:
- amplitudes: float32 [768, 768], P('rows'), may hold values from -6 to 6
- left_terms: float32 [8, 768, 768], P('terms', 'rows'), may hold values from -0.078125 to 0.078125
- right_terms: float32 [8, 768, 768], P('terms'), may hold values from -0.21875 to 0.21875
- source_list: int32 [8, 4], replicated, may hold values from 0 to 7, as said below
- list_count: int32 [8], replicated, may hold values from 1 to 4
- weight_index: int32 [8, 4], replicated, may hold values from 0 to 7
- weight_table: float32 [8], replicated, may hold values from -4 to 4
Outputs:
- isometry: float32 [768, 768], P('rows')
- new_environment: float32 [8, 768, 768], P('terms', 'rows')
The draws below stay inside these ranges and needn't reach their ends.
Inputs may be any that keep to these rules, and one draw needn't show every extreme that they name: `source_list`: every block id appears in column 0 exactly once.
All inputs are finite; a program needn't handle non-finite values.
Results may differ from the reference program's by a relative error of at most 0.00016.
Values sent between devices are 32-bit elements; how exact they have to be, the bound alone decides.
No kernel may reach another device: no remote copies, remote signals or barrier semaphores. Data moves between devices by JAX's collectives and lax.ppermute only.
A program may use at most 64 MiB of HBM per device.

```python
import math
import jax
import jax.numpy as jnp
from jax import lax

K = 768
FAN = 4
NCOEF = 8
SWEEPS = 3
TERMS = 8


def draw_source_list(key, part):
    first_key, other_key = jax.random.split(jax.random.fold_in(key, 11))
    leading = jax.random.permutation(first_key, TERMS).astype(jnp.int32)
    others = jax.random.randint(other_key, (TERMS, FAN - 1), 0, TERMS).astype(jnp.int32)
    return jnp.concatenate([leading[:, None], others], axis=1).astype(jnp.int32)


def draw_list_count(key, part):
    count_key, place_key = jax.random.split(jax.random.fold_in(key, 23))
    counts = jax.random.randint(count_key, (TERMS,), 1, FAN + 1).astype(jnp.int32)
    places = jax.random.permutation(place_key, TERMS)
    counts = counts.at[places[0]].set(FAN)
    counts = counts.at[places[1]].set(1)
    return counts.astype(jnp.int32)


def draw_weight_index(key, part):
    first_key, other_key = jax.random.split(jax.random.fold_in(key, 37))
    leading = (jax.random.permutation(first_key, TERMS) % NCOEF).astype(jnp.int32)
    others = jax.random.randint(other_key, (TERMS, FAN - 1), 0, NCOEF).astype(jnp.int32)
    return jnp.concatenate([leading[:, None], others], axis=1).astype(jnp.int32)


def block_levels(rng, extent, shards, smallest, largest):
    gain = 1.0
    for position, blocks in shards:
        steps = jax.random.uniform(jax.random.fold_in(jax.random.fold_in(rng, 6), position), (blocks,), jnp.float32, smallest / len(shards), largest / len(shards))
        gain = gain * jnp.repeat(jnp.exp(steps), extent[position] // blocks).reshape((-1,) + (1,) * (len(extent) - 1 - position))
    return gain


def centred(key, dims, scale, bound, cuts=(), held_as=jnp.bfloat16):
    result = jax.random.normal(key, dims, jnp.float32) * scale
    if len(cuts) > 0:
        result = block_levels(key, dims, cuts, -0.22, 0.18) * result
    return jnp.clip(result, min=-bound, max=bound).astype(held_as)


def setup_inputs(seed: int = 0) -> dict:
    keys = jax.random.split(jax.random.key(seed), 8)
    return {
        "amplitudes": centred(keys[0], (K, K), 1.0, 6.0, ((0, 4),), jnp.float32),
        "left_terms": centred(keys[1], (TERMS, K, K), (K * TERMS) ** -0.5, 0.078125, ((0, 8), (1, 4)), jnp.float32),
        "right_terms": centred(keys[2], (TERMS, K, K), K ** -0.5, 0.21875, ((0, 8),), jnp.float32),
        "source_list": draw_source_list(jax.random.fold_in(keys[7], 71), 0),
        "list_count": draw_list_count(jax.random.fold_in(keys[7], 71), 0),
        "weight_index": draw_weight_index(jax.random.fold_in(keys[7], 71), 0),
        "weight_table": centred(keys[6], (NCOEF,), 1.0, 4.0, (), jnp.float32),
    }


HIGH = lax.Precision.HIGHEST
COEF_ONE = 3.4445
COEF_TWO = -4.775
COEF_THREE = 2.0315

def apply_terms(amplitudes, left_terms, right_terms):

    def accumulate(summed, pair):
        left_block, right_block = pair
        mapped = jnp.dot(left_block, amplitudes, precision=HIGH, preferred_element_type=jnp.float32)
        return (summed + jnp.dot(mapped, right_block, precision=HIGH, preferred_element_type=jnp.float32), None)
    summed, _ = lax.scan(accumulate, jnp.zeros(amplitudes.shape, jnp.float32), (left_terms, right_terms))
    return amplitudes - 0.3 * summed

def combination(source_list, list_count, weight_index, weight_table):
    in_use = (jnp.arange(FAN)[None, :] < list_count[:, None]).astype(jnp.float32)
    picked = (weight_index[:, :, None] == jnp.arange(NCOEF)[None, None, :]).astype(jnp.float32)
    weights = jnp.einsum('jcn,n->jc', picked, weight_table.astype(jnp.float32), precision=HIGH) * in_use
    matches = (source_list[:, :, None] == jnp.arange(TERMS)[None, None, :]).astype(jnp.float32)
    return jnp.einsum('jc,jcb->jb', weights, matches, precision=HIGH)

def reference(amplitudes, left_terms, right_terms, source_list, list_count, weight_index, weight_table):
    first = apply_terms(amplitudes, left_terms, right_terms)
    second = apply_terms(first, left_terms, right_terms)
    squares = jnp.sum(second * second)
    iterate = second / jnp.sqrt(squares)
    for repeat in range(SWEEPS):
        gram_matrix = jnp.dot(iterate.T, iterate, precision=HIGH, preferred_element_type=jnp.float32)
        once = jnp.dot(iterate, gram_matrix, precision=HIGH, preferred_element_type=jnp.float32)
        twice = jnp.dot(once, gram_matrix, precision=HIGH, preferred_element_type=jnp.float32)
        iterate = COEF_ONE * iterate + COEF_TWO * once + COEF_THREE * twice
    isometry = math.sqrt(K) * iterate
    mixing = combination(source_list, list_count, weight_index, weight_table)

    def one_block(weights):
        combined = jnp.einsum('b,bkl->kl', weights, left_terms, precision=HIGH)
        rotated = jnp.dot(combined, isometry, precision=HIGH, preferred_element_type=jnp.float32)
        return jnp.dot(isometry.T, rotated, precision=HIGH, preferred_element_type=jnp.float32)
    new_environment = lax.map(one_block, mixing)
    return (isometry, new_environment)
```

```python
import functools
import math

import jax
import jax.numpy as jnp
from jax import lax
from jax.experimental import pallas as pl
from jax.experimental.pallas import tpu as pltpu
from jax.sharding import PartitionSpec as P

SWEEPS = 3

HIGH = lax.Precision.HIGHEST
COEF_ONE = 3.4445
COEF_TWO = -4.775
COEF_THREE = 2.0315
STEP = 0.3


ANY = pl.BlockSpec(memory_space=pl.ANY)
VMEM = pl.BlockSpec(memory_space=pltpu.VMEM)
SMEM = pl.BlockSpec(memory_space=pltpu.SMEM)
BF16 = jnp.bfloat16
F32 = jnp.float32


def halves(value):
    high = value.astype(BF16)
    low = (value - high.astype(F32)).astype(BF16)
    return high, low


def product(left, right, over=(1, 0)):
    dims = (((over[0],), (over[1],)), ((), ()))
    dot = functools.partial(lax.dot_general, dimension_numbers=dims, preferred_element_type=F32)
    return dot(left[0], right[0]) + (dot(left[0], right[1]) + dot(left[1], right[0]))


def shape(dims, dtype=F32):
    return jax.ShapeDtypeStruct(dims, dtype)


class Places:
    def __init__(self, terms, rows, slab):
        self.terms, self.rows, self.slab = terms, rows, slab
        self.cores = 2
        self.chips = terms // self.cores
        self.piece = slab // terms
        self.half = slab // self.cores

    def here(self):
        term = lax.axis_index("terms")
        return term // self.cores, term % self.cores, lax.axis_index("rows")

    def swap(self, value, chip=0, core=0, row=0):
        pairs = []
        for term in range(self.terms):
            for line in range(self.rows):
                other = term ^ (chip * self.cores + core)
                pairs.append((term * self.rows + line, other * self.rows + (line ^ row)))
        return lax.ppermute(value, ("terms", "rows"), pairs)


def prepare(places, left, right):
    width = left.shape[1]
    piece, half = places.piece, places.half

    def kernel(left_ref, right_ref, lh_ref, ll_ref, rh_ref, rl_ref, ordered):
        chip, core, _ = places.here()
        for side in range(places.cores):
            for slot in range(places.chips):
                source = (core ^ side) * half + (chip ^ slot) * piece
                source = pl.multiple_of(source, 8)
                ordered[pl.ds(side * half + slot * piece, piece), :] = left_ref[pl.ds(source, piece), :]
        lh_ref[...], ll_ref[...] = halves(ordered[...])
        rh_ref[...], rl_ref[...] = halves(right_ref[...])

    return pl.pallas_call(
        kernel,
        out_shape=(shape(left.shape, BF16),) * 2 + (shape(right.shape, BF16),) * 2,
        in_specs=[VMEM, VMEM],
        out_specs=(VMEM,) * 4,
        scratch_shapes=[pltpu.VMEM(left.shape, F32)],
        name="prepare",
    )(left, right)


def assemble(places, layout, parts, whole, sem):
    chip, core, line = places.here()
    copies = []
    for (chip_slot, core_slot, row_slots, rows_each, base), part in zip(layout, parts):
        for index, row_slot in enumerate(row_slots):
            if rows_each == places.slab:
                start = (line ^ row_slot) * places.slab
            else:
                start = (
                    (line ^ row_slot) * places.slab
                    + (core ^ core_slot) * places.half
                    + (chip ^ chip_slot) * places.piece
                )
            start = pl.multiple_of(start, 8)
            copies.append(
                pltpu.make_async_copy(
                    part.at[pl.ds(index * rows_each, rows_each), :],
                    whole.at[pl.ds(start, rows_each), :],
                    sem.at[len(copies)],
                )
            )
    for copy in copies:
        copy.start()
    for copy in copies:
        copy.wait()


def semaphores(layout):
    return pltpu.SemaphoreType.DMA((sum(len(entry[2]) for entry in layout),))


def apply_terms(places, layout, parts, prepared):
    width = parts[0].shape[1]
    half = places.half

    def kernel(*refs):
        count = len(parts)
        lh_ref, ll_ref, rh_ref, rl_ref, keep_ref, send_ref, whole, sem = refs[count:]
        assemble(places, layout, refs[:count], whole, sem)
        mapped = product((lh_ref[...], ll_ref[...]), halves(whole[...]))
        total = product(halves(mapped), (rh_ref[...], rl_ref[...]))
        keep_ref[...] = total[:half]
        send_ref[...] = total[half:]

    return pl.pallas_call(
        kernel,
        out_shape=(shape((half, width)),) * 2,
        in_specs=[ANY] * len(parts) + [VMEM] * 4,
        out_specs=(VMEM, VMEM),
        scratch_shapes=[pltpu.VMEM((width, width), F32), semaphores(layout)],
        name="apply",
    )(*parts, *prepared)


def add_pieces(places, keep, received):
    piece = places.piece
    width = keep.shape[1]

    def kernel(keep_ref, received_ref, *outs):
        for slot, out in enumerate(outs):
            rows = pl.ds(slot * piece, piece)
            out[...] = keep_ref[rows, :] + received_ref[rows, :]

    return pl.pallas_call(
        kernel,
        out_shape=(shape((piece, width)),) * places.chips,
        in_specs=[VMEM, VMEM],
        out_specs=(VMEM,) * places.chips,
        name="add_pieces",
    )(keep, received)


def step_piece(base, pieces):
    def kernel(base_ref, *refs):
        total = refs[0][...]
        for ref in refs[1:-1]:
            total = total + ref[...]
        refs[-1][...] = base_ref[...] - STEP * total

    return pl.pallas_call(
        kernel,
        out_shape=shape(base.shape),
        in_specs=[VMEM] * (1 + len(pieces)),
        out_specs=VMEM,
        name="step_piece",
    )(base, *pieces)


def stack(parts):
    width = parts[0].shape[1]
    heights = [part.shape[0] for part in parts]

    def kernel(*refs):
        out = refs[-1]
        start = 0
        for ref, height in zip(refs[:-1], heights):
            out[pl.ds(start, height), :] = ref[...]
            start += height

    return pl.pallas_call(
        kernel,
        out_shape=shape((sum(heights), width)),
        in_specs=[VMEM] * len(parts),
        out_specs=VMEM,
        name="stack",
    )(*parts)


def spread(places, piece, with_own=True):
    lines = [places.swap(piece, row=slot) for slot in range(1, places.rows)]
    slots = list(range(1, places.rows))
    if with_own:
        lines = [piece] + lines
        slots = [0] + slots
    mine = stack(lines)
    chips = [mine] + [places.swap(mine, chip=slot) for slot in range(1, places.chips)]
    layout, parts = [], []
    for core_slot in range(places.cores):
        for slot, part in enumerate(chips):
            layout.append((slot, core_slot, slots, places.piece, 0))
            parts.append(places.swap(part, core=core_slot) if core_slot else part)
    return layout, parts


def reduced(places, keep, send):
    received = places.swap(send, core=1)
    own, *others = add_pieces(places, keep, received)
    return [own] + [places.swap(part, chip=slot + 1) for slot, part in enumerate(others)]


def orthogonal(places, layout, parts):
    width = parts[0].shape[1]
    slab = places.slab
    tile = 256 if width % 256 == 0 else width
    blocks = width // tile

    def symmetric(out, compute):
        for i in range(blocks):
            strip = compute(i)
            out[pl.ds(i * tile, tile), pl.ds(i * tile, width - i * tile)] = strip
            for j in range(i + 1, blocks):
                out[pl.ds(j * tile, tile), pl.ds(i * tile, tile)] = strip[
                    :, (j - i) * tile : (j - i + 1) * tile
                ].T

    def kernel(*refs):
        count = len(parts)
        slab_ref, high_ref, low_ref, iterate, gram, gram_squared, sem = refs[count:]
        assemble(places, layout, refs[:count], iterate, sem)
        values = iterate[...]
        values = values * (1.0 / jnp.sqrt(jnp.sum(values * values)))
        iterate[...] = values
        for repeat in range(SWEEPS):
            xh, xl = halves(iterate[...])

            def gram_strip(i):
                cols = slice(i * tile, (i + 1) * tile)
                return product(
                    (xh[:, cols], xl[:, cols]), (xh[:, i * tile :], xl[:, i * tile :]), (0, 0)
                )

            symmetric(gram, gram_strip)
            gh, gl = halves(gram[...])

            def square_strip(i):
                rows = slice(i * tile, (i + 1) * tile)
                return product((gh[rows], gl[rows]), (gh[:, i * tile :], gl[:, i * tile :]))

            symmetric(gram_squared, square_strip)
            poly = halves(COEF_TWO * gram[...] + COEF_THREE * gram_squared[...])
            iterate[...] = COEF_ONE * iterate[...] + product((xh, xl), poly)
        final = math.sqrt(width) * iterate[...]
        iterate[...] = final
        high_ref[...], low_ref[...] = halves(final)
        line = lax.axis_index("rows")
        slab_ref[...] = iterate[pl.ds(pl.multiple_of(line * slab, 8), slab), :]

    return pl.pallas_call(
        kernel,
        out_shape=(shape((slab, width)),) + (shape((width, width), BF16),) * 2,
        in_specs=[ANY] * len(parts),
        out_specs=(VMEM,) * 3,
        scratch_shapes=[pltpu.VMEM((width, width), F32)] * 3 + [semaphores(layout)],
        name="orthogonal",
    )(*parts)


def environment(places, layout, parts, high, low, slab_high, slab_low):
    width = high.shape[0]
    slab = places.slab

    def kernel(*refs):
        count = len(parts)
        high_ref, low_ref, sh_ref, sl_ref, out_ref, whole, sem = refs[count:]
        assemble(places, layout, refs[:count], whole, sem)
        rotated = product((sh_ref[...], sl_ref[...]), halves(whole[...]), (0, 0))
        out_ref[...] = product(halves(rotated), (high_ref[...], low_ref[...]))

    return pl.pallas_call(
        kernel,
        out_shape=shape((slab, width)),
        in_specs=[ANY] * len(parts) + [VMEM] * 4,
        out_specs=VMEM,
        scratch_shapes=[pltpu.VMEM((width, width), F32), semaphores(layout)],
        name="environment",
    )(*parts, high, low, slab_high, slab_low)


def combine_pieces(pieces, source_list, list_count, weight_index, weight_table):
    fan = source_list.shape[1]

    def kernel(source_ref, count_ref, index_ref, table_ref, pieces_ref, out_ref):
        for j in range(source_list.shape[0]):
            total = None
            for c in range(fan):
                weight = jnp.where(c < count_ref[j], table_ref[index_ref[j, c]], 0.0)
                term = weight * pieces_ref[source_ref[j, c]]
                total = term if total is None else total + term
            out_ref[j] = total

    return pl.pallas_call(
        kernel,
        out_shape=shape((source_list.shape[0],) + pieces.shape[1:]),
        in_specs=[SMEM] * 4 + [VMEM],
        out_specs=VMEM,
        name="combine",
    )(source_list, list_count, weight_index, weight_table, pieces)


def combined_slab(left, source_list, list_count, weight_index, weight_table):
    rows, width = left.shape
    owners = lax.axis_size("terms")
    if rows % (8 * owners) == 0:
        run = (rows // owners, width)
    else:
        run = (1, rows * width // owners)
    pieces = lax.all_to_all(left.reshape((owners,) + run), "terms", 0, 0, tiled=True)
    mixed = combine_pieces(pieces, source_list, list_count, weight_index, weight_table)
    return lax.all_to_all(mixed, "terms", 0, 0, tiled=True).reshape(rows, width)


def body(amplitudes, left_terms, right_terms, source_list, list_count, weight_index, weight_table):
    left, right = left_terms[0], right_terms[0]
    slab, width = left.shape
    terms, rows = lax.axis_size("terms"), lax.axis_size("rows")
    places = Places(terms, rows, slab)
    swaps = terms % 2 == 0 and terms <= 8 and terms & (terms - 1) == 0 and rows & (rows - 1) == 0
    swaps = swaps and slab % (8 * terms) == 0

    combined = combined_slab(left, source_list, list_count, weight_index, weight_table)
    chip, core, line = places.here()
    every = list(range(rows))
    slabs = [(0, 0, [slot], slab, 0) for slot in every]
    if swaps:
        prepared = prepare(places, left, right)
        start = core * places.half + chip * places.piece
        base = lax.dynamic_slice_in_dim(amplitudes, start, places.piece, 0)
        layout, parts = spread(places, base, with_own=False)
        layout, parts = [slabs[0]] + layout, [amplitudes] + parts
        for _ in range(2):
            keep, send = apply_terms(places, layout, parts, prepared)
            base = step_piece(base, reduced(places, keep, send))
            layout, parts = spread(places, base)
        blocks = [combined] + [places.swap(combined, row=slot) for slot in every[1:]]
    else:
        matrix = amplitudes
        for _ in range(2):
            full = lax.all_gather(matrix, "rows", axis=0, tiled=True)
            mapped = jnp.dot(left, full, precision=HIGH)
            summed = lax.psum(jnp.dot(mapped, right, precision=HIGH), "terms")
            matrix = matrix - STEP * summed
        full = lax.all_gather(matrix, "rows", axis=0, tiled=True)
        layout = slabs
        parts = [lax.dynamic_slice_in_dim(full, (line ^ slot) * slab, slab, 0) for slot in every]
        full = lax.all_gather(combined, "rows", axis=0, tiled=True)
        blocks = [lax.dynamic_slice_in_dim(full, (line ^ slot) * slab, slab, 0) for slot in every]
    isometry, high, low = orthogonal(places, layout, parts)
    slab_high = lax.dynamic_slice_in_dim(high, line * slab, slab, 1)
    slab_low = lax.dynamic_slice_in_dim(low, line * slab, slab, 1)
    new_environment = environment(places, slabs, blocks, high, low, slab_high, slab_low)
    return (isometry, new_environment[None])


def solution(mesh):
    placed = (P("rows", None), P("terms", "rows", None), P("terms", None, None), P(), P(), P(), P())
    return jax.shard_map(
        body,
        mesh=mesh,
        in_specs=placed,
        out_specs=(P("rows", None), P("terms", "rows", None)),
        check_vma=False,
    )
```

```python
import functools
import math

import jax
import jax.numpy as jnp
from jax import lax
from jax.experimental import pallas as pl
from jax.experimental.pallas import tpu as pltpu
from jax.sharding import PartitionSpec as P

SWEEPS = 3

HIGH = lax.Precision.HIGHEST
COEF_ONE = 3.4445
COEF_TWO = -4.775
COEF_THREE = 2.0315
STEP = 0.3


ANY = pl.BlockSpec(memory_space=pl.ANY)
VMEM = pl.BlockSpec(memory_space=pltpu.VMEM)
SMEM = pl.BlockSpec(memory_space=pltpu.SMEM)
MIB = 1 << 20
BF16 = jnp.bfloat16
F32 = jnp.float32


def halves(value):
    high = value.astype(BF16)
    low = (value - high.astype(F32)).astype(BF16)
    return high, low


def product(left, right, over=(1, 0)):
    dims = (((over[0],), (over[1],)), ((), ()))
    dot = functools.partial(lax.dot_general, dimension_numbers=dims, preferred_element_type=F32)
    return dot(left[0], right[0]) + (dot(left[0], right[1]) + dot(left[1], right[0]))


def shape(dims, dtype=F32):
    return jax.ShapeDtypeStruct(dims, dtype)


class Places:
    def __init__(self, terms, rows, slab):
        self.terms, self.rows, self.slab = terms, rows, slab
        self.cores = 2
        self.chips = terms // self.cores
        self.piece = slab // terms
        self.half = slab // self.cores

    def here(self):
        term = lax.axis_index("terms")
        return term // self.cores, term % self.cores, lax.axis_index("rows")

    def swap(self, value, chip=0, core=0, row=0):
        pairs = []
        for term in range(self.terms):
            for line in range(self.rows):
                other = term ^ (chip * self.cores + core)
                pairs.append((term * self.rows + line, other * self.rows + (line ^ row)))
        return lax.ppermute(value, ("terms", "rows"), pairs)


def prepare(places, left, right):
    width = left.shape[1]
    piece, half = places.piece, places.half

    def kernel(left_ref, right_ref, lh_ref, ll_ref, rh_ref, rl_ref, ordered):
        chip, core, _ = places.here()
        for side in range(places.cores):
            for slot in range(places.chips):
                source = (core ^ side) * half + (chip ^ slot) * piece
                source = pl.multiple_of(source, 8)
                ordered[pl.ds(side * half + slot * piece, piece), :] = left_ref[pl.ds(source, piece), :]
        lh_ref[...], ll_ref[...] = halves(ordered[...])
        rh_ref[...], rl_ref[...] = halves(right_ref[...])

    return pl.pallas_call(
        kernel,
        out_shape=(shape(left.shape, BF16),) * 2 + (shape(right.shape, BF16),) * 2,
        in_specs=[VMEM, VMEM],
        out_specs=(VMEM,) * 4,
        scratch_shapes=[pltpu.VMEM(left.shape, F32)],
        compiler_params=pltpu.CompilerParams(vmem_limit_bytes=12 * MIB),
        name="prepare",
    )(left, right)


def assemble(places, layout, parts, whole, sem):
    chip, core, line = places.here()
    copies = []
    for (chip_slot, core_slot, row_slots, rows_each, base), part in zip(layout, parts):
        for index, row_slot in enumerate(row_slots):
            if rows_each == places.slab:
                start = (line ^ row_slot) * places.slab
            else:
                start = (
                    (line ^ row_slot) * places.slab
                    + (core ^ core_slot) * places.half
                    + (chip ^ chip_slot) * places.piece
                )
            start = pl.multiple_of(start, 8)
            copies.append(
                pltpu.make_async_copy(
                    part.at[pl.ds(index * rows_each, rows_each), :],
                    whole.at[pl.ds(start, rows_each), :],
                    sem.at[len(copies)],
                )
            )
    for copy in copies:
        copy.start()
    for copy in copies:
        copy.wait()


def semaphores(layout):
    return pltpu.SemaphoreType.DMA((sum(len(entry[2]) for entry in layout),))


def apply_terms(places, layout, parts, prepared):
    width = parts[0].shape[1]
    half = places.half

    def kernel(*refs):
        count = len(parts)
        lh_ref, ll_ref, rh_ref, rl_ref, keep_ref, send_ref, whole, sem = refs[count:]
        assemble(places, layout, refs[:count], whole, sem)
        mapped = product((lh_ref[...], ll_ref[...]), halves(whole[...]))
        total = product(halves(mapped), (rh_ref[...], rl_ref[...]))
        keep_ref[...] = total[:half]
        send_ref[...] = total[half:]

    return pl.pallas_call(
        kernel,
        out_shape=(shape((half, width)),) * 2,
        in_specs=[ANY] * len(parts) + [VMEM] * 4,
        out_specs=(VMEM, VMEM),
        scratch_shapes=[pltpu.VMEM((width, width), F32), semaphores(layout)],
        compiler_params=pltpu.CompilerParams(vmem_limit_bytes=16 * MIB),
        name="apply",
    )(*parts, *prepared)


def add_pieces(places, keep, received):
    piece = places.piece
    width = keep.shape[1]

    def kernel(keep_ref, received_ref, *outs):
        for slot, out in enumerate(outs):
            rows = pl.ds(slot * piece, piece)
            out[...] = keep_ref[rows, :] + received_ref[rows, :]

    return pl.pallas_call(
        kernel,
        out_shape=(shape((piece, width)),) * places.chips,
        in_specs=[VMEM, VMEM],
        out_specs=(VMEM,) * places.chips,
        compiler_params=pltpu.CompilerParams(vmem_limit_bytes=2 * MIB),
        name="add_pieces",
    )(keep, received)


def step_piece(base, pieces):
    def kernel(base_ref, *refs):
        total = refs[0][...]
        for ref in refs[1:-1]:
            total = total + ref[...]
        refs[-1][...] = base_ref[...] - STEP * total

    return pl.pallas_call(
        kernel,
        out_shape=shape(base.shape),
        in_specs=[VMEM] * (1 + len(pieces)),
        out_specs=VMEM,
        compiler_params=pltpu.CompilerParams(vmem_limit_bytes=2 * MIB),
        name="step_piece",
    )(base, *pieces)


def stack(parts):
    width = parts[0].shape[1]
    heights = [part.shape[0] for part in parts]

    def kernel(*refs):
        out = refs[-1]
        start = 0
        for ref, height in zip(refs[:-1], heights):
            out[pl.ds(start, height), :] = ref[...]
            start += height

    return pl.pallas_call(
        kernel,
        out_shape=shape((sum(heights), width)),
        in_specs=[VMEM] * len(parts),
        out_specs=VMEM,
        compiler_params=pltpu.CompilerParams(vmem_limit_bytes=2 * MIB),
        name="stack",
    )(*parts)


def spread(places, piece, with_own=True):
    lines = [places.swap(piece, row=slot) for slot in range(1, places.rows)]
    slots = list(range(1, places.rows))
    if with_own:
        lines = [piece] + lines
        slots = [0] + slots
    mine = stack(lines)
    chips = [mine] + [places.swap(mine, chip=slot) for slot in range(1, places.chips)]
    layout, parts = [], []
    for core_slot in range(places.cores):
        for slot, part in enumerate(chips):
            layout.append((slot, core_slot, slots, places.piece, 0))
            parts.append(places.swap(part, core=core_slot) if core_slot else part)
    return layout, parts


def reduced(places, keep, send):
    received = places.swap(send, core=1)
    own, *others = add_pieces(places, keep, received)
    return [own] + [places.swap(part, chip=slot + 1) for slot, part in enumerate(others)]


def orthogonal(places, layout, parts):
    width = parts[0].shape[1]
    slab = places.slab
    tile = 256 if width % 256 == 0 else width
    blocks = width // tile

    def symmetric(out, compute):
        for i in range(blocks):
            strip = compute(i)
            out[pl.ds(i * tile, tile), pl.ds(i * tile, width - i * tile)] = strip
            for j in range(i + 1, blocks):
                out[pl.ds(j * tile, tile), pl.ds(i * tile, tile)] = strip[
                    :, (j - i) * tile : (j - i + 1) * tile
                ].T

    def kernel(*refs):
        count = len(parts)
        slab_ref, high_ref, low_ref, iterate, gram, gram_squared, sem = refs[count:]
        assemble(places, layout, refs[:count], iterate, sem)
        values = iterate[...]
        values = values * (1.0 / jnp.sqrt(jnp.sum(values * values)))
        iterate[...] = values
        for repeat in range(SWEEPS):
            xh, xl = halves(iterate[...])

            def gram_strip(i):
                cols = slice(i * tile, (i + 1) * tile)
                return product(
                    (xh[:, cols], xl[:, cols]), (xh[:, i * tile :], xl[:, i * tile :]), (0, 0)
                )

            symmetric(gram, gram_strip)
            gh, gl = halves(gram[...])

            def square_strip(i):
                rows = slice(i * tile, (i + 1) * tile)
                return product((gh[rows], gl[rows]), (gh[:, i * tile :], gl[:, i * tile :]))

            symmetric(gram_squared, square_strip)
            poly = halves(COEF_TWO * gram[...] + COEF_THREE * gram_squared[...])
            iterate[...] = COEF_ONE * iterate[...] + product((xh, xl), poly)
        final = math.sqrt(width) * iterate[...]
        iterate[...] = final
        high_ref[...], low_ref[...] = halves(final)
        line = lax.axis_index("rows")
        slab_ref[...] = iterate[pl.ds(pl.multiple_of(line * slab, 8), slab), :]

    return pl.pallas_call(
        kernel,
        out_shape=(shape((slab, width)),) + (shape((width, width), BF16),) * 2,
        in_specs=[ANY] * len(parts),
        out_specs=(VMEM,) * 3,
        scratch_shapes=[pltpu.VMEM((width, width), F32)] * 3 + [semaphores(layout)],
        compiler_params=pltpu.CompilerParams(vmem_limit_bytes=40 * MIB),
        name="orthogonal",
    )(*parts)


def environment(places, layout, parts, high, low, slab_high, slab_low):
    width = high.shape[0]
    slab = places.slab

    def kernel(*refs):
        count = len(parts)
        high_ref, low_ref, sh_ref, sl_ref, out_ref, whole, sem = refs[count:]
        assemble(places, layout, refs[:count], whole, sem)
        rotated = product((sh_ref[...], sl_ref[...]), halves(whole[...]), (0, 0))
        out_ref[...] = product(halves(rotated), (high_ref[...], low_ref[...]))

    return pl.pallas_call(
        kernel,
        out_shape=shape((slab, width)),
        in_specs=[ANY] * len(parts) + [VMEM] * 4,
        out_specs=VMEM,
        scratch_shapes=[pltpu.VMEM((width, width), F32), semaphores(layout)],
        compiler_params=pltpu.CompilerParams(vmem_limit_bytes=16 * MIB),
        name="environment",
    )(*parts, high, low, slab_high, slab_low)


def combine_pieces(pieces, source_list, list_count, weight_index, weight_table):
    fan = source_list.shape[1]

    def kernel(source_ref, count_ref, index_ref, table_ref, pieces_ref, out_ref):
        for j in range(source_list.shape[0]):
            total = None
            for c in range(fan):
                weight = jnp.where(c < count_ref[j], table_ref[index_ref[j, c]], 0.0)
                term = weight * pieces_ref[source_ref[j, c]]
                total = term if total is None else total + term
            out_ref[j] = total

    return pl.pallas_call(
        kernel,
        out_shape=shape((source_list.shape[0],) + pieces.shape[1:]),
        in_specs=[SMEM] * 4 + [VMEM],
        out_specs=VMEM,
        compiler_params=pltpu.CompilerParams(vmem_limit_bytes=4 * MIB),
        name="combine",
    )(source_list, list_count, weight_index, weight_table, pieces)


def combined_slab(left, source_list, list_count, weight_index, weight_table):
    rows, width = left.shape
    owners = lax.axis_size("terms")
    if rows % (8 * owners) == 0:
        run = (rows // owners, width)
    else:
        run = (1, rows * width // owners)
    pieces = lax.all_to_all(left.reshape((owners,) + run), "terms", 0, 0, tiled=True)
    mixed = combine_pieces(pieces, source_list, list_count, weight_index, weight_table)
    return lax.all_to_all(mixed, "terms", 0, 0, tiled=True).reshape(rows, width)


def body(amplitudes, left_terms, right_terms, source_list, list_count, weight_index, weight_table):
    left, right = left_terms[0], right_terms[0]
    slab, width = left.shape
    terms, rows = lax.axis_size("terms"), lax.axis_size("rows")
    places = Places(terms, rows, slab)
    swaps = terms % 2 == 0 and terms <= 8 and terms & (terms - 1) == 0 and rows & (rows - 1) == 0
    swaps = swaps and slab % (8 * terms) == 0

    combined = combined_slab(left, source_list, list_count, weight_index, weight_table)
    chip, core, line = places.here()
    every = list(range(rows))
    slabs = [(0, 0, [slot], slab, 0) for slot in every]
    if swaps:
        prepared = prepare(places, left, right)
        start = core * places.half + chip * places.piece
        base = lax.dynamic_slice_in_dim(amplitudes, start, places.piece, 0)
        layout, parts = spread(places, base, with_own=False)
        layout, parts = [slabs[0]] + layout, [amplitudes] + parts
        for _ in range(2):
            keep, send = apply_terms(places, layout, parts, prepared)
            base = step_piece(base, reduced(places, keep, send))
            layout, parts = spread(places, base)
        blocks = [combined] + [places.swap(combined, row=slot) for slot in every[1:]]
    else:
        matrix = amplitudes
        for _ in range(2):
            full = lax.all_gather(matrix, "rows", axis=0, tiled=True)
            mapped = jnp.dot(left, full, precision=HIGH)
            summed = lax.psum(jnp.dot(mapped, right, precision=HIGH), "terms")
            matrix = matrix - STEP * summed
        full = lax.all_gather(matrix, "rows", axis=0, tiled=True)
        layout = slabs
        parts = [lax.dynamic_slice_in_dim(full, (line ^ slot) * slab, slab, 0) for slot in every]
        full = lax.all_gather(combined, "rows", axis=0, tiled=True)
        blocks = [lax.dynamic_slice_in_dim(full, (line ^ slot) * slab, slab, 0) for slot in every]
    isometry, high, low = orthogonal(places, layout, parts)
    slab_high = lax.dynamic_slice_in_dim(high, line * slab, slab, 1)
    slab_low = lax.dynamic_slice_in_dim(low, line * slab, slab, 1)
    new_environment = environment(places, slabs, blocks, high, low, slab_high, slab_low)
    return (isometry, new_environment[None])


def solution(mesh):
    placed = (P("rows", None), P("terms", "rows", None), P("terms", None, None), P(), P(), P(), P())
    return jax.shard_map(
        body,
        mesh=mesh,
        in_specs=placed,
        out_specs=(P("rows", None), P("terms", "rows", None)),
        check_vma=False,
    )
```

```python
import functools
import math

import jax
import jax.numpy as jnp
from jax import lax
from jax.experimental import pallas as pl
from jax.experimental.pallas import tpu as pltpu
from jax.sharding import PartitionSpec as P


SWEEPS = 3

HIGH = lax.Precision.HIGHEST
COEF_ONE = 3.4445
COEF_TWO = -4.775
COEF_THREE = 2.0315
STEP = 0.3


VMEM = pl.BlockSpec(memory_space=pltpu.VMEM)
SMEM = pl.BlockSpec(memory_space=pltpu.SMEM)
MIB = 1 << 20
BF16 = jnp.bfloat16
F32 = jnp.float32


def halves(value):
    high = value.astype(BF16)
    low = (value - high.astype(F32)).astype(BF16)
    return high, low


def product(left, right, over=(1, 0)):
    dims = (((over[0],), (over[1],)), ((), ()))
    dot = functools.partial(lax.dot_general, dimension_numbers=dims, preferred_element_type=F32)
    return dot(left[0], right[0]) + (dot(left[0], right[1]) + dot(left[1], right[0]))


def shape(dims, dtype=F32):
    return jax.ShapeDtypeStruct(dims, dtype)


class Places:
    def __init__(self, terms, rows, slab):
        self.terms, self.rows, self.slab = terms, rows, slab
        self.cores = 2
        self.chips = terms // self.cores
        self.piece = slab // terms
        self.half = slab // self.cores

    def here(self):
        term = lax.axis_index("terms")
        return term // self.cores, term % self.cores, lax.axis_index("rows")

    def swap(self, value, chip=0, core=0, row=0):
        pairs = []
        for term in range(self.terms):
            for line in range(self.rows):
                other = term ^ (chip * self.cores + core)
                pairs.append((term * self.rows + line, other * self.rows + (line ^ row)))
        return lax.ppermute(value, ("terms", "rows"), pairs)


def prepare(places, left, right):
    piece, half = places.piece, places.half

    def kernel(left_ref, right_ref, lh_ref, ll_ref, rh_ref, rl_ref, ordered):
        chip, core, _ = places.here()
        for side in range(places.cores):
            for slot in range(places.chips):
                source = (core ^ side) * half + (chip ^ slot) * piece
                source = pl.multiple_of(source, 8)
                ordered[pl.ds(side * half + slot * piece, piece), :] = left_ref[pl.ds(source, piece), :]
        lh_ref[...], ll_ref[...] = halves(ordered[...])
        rh_ref[...], rl_ref[...] = halves(right_ref[...])

    return pl.pallas_call(
        kernel,
        out_shape=(shape(left.shape, BF16),) * 2 + (shape(right.shape, BF16),) * 2,
        in_specs=[VMEM, VMEM],
        out_specs=(VMEM,) * 4,
        scratch_shapes=[pltpu.VMEM(left.shape, F32)],
        compiler_params=pltpu.CompilerParams(vmem_limit_bytes=12 * MIB),
        name="prepare",
    )(left, right)


def assemble(places, layout, parts, store):
    chip, core, line = places.here()
    for (chip_slot, core_slot, row_slots, rows_each), part in zip(layout, parts):
        for index, row_slot in enumerate(row_slots):
            start = (line ^ row_slot) * places.slab
            if rows_each != places.slab:
                start = start + (core ^ core_slot) * places.half + (chip ^ chip_slot) * places.piece
            store(pl.multiple_of(start, 8), rows_each, part[pl.ds(index * rows_each, rows_each), :])


def put_in(whole):
    def store(start, height, value):
        whole[pl.ds(start, height), :] = value

    return store


def apply_terms(places, layout, parts, prepared):
    width = parts[0].shape[1]
    half = places.half

    def kernel(*refs):
        count = len(parts)
        lh_ref, ll_ref, rh_ref, rl_ref, keep_ref, send_ref, whole = refs[count:]
        assemble(places, layout, refs[:count], put_in(whole))
        mapped = product((lh_ref[...], ll_ref[...]), halves(whole[...]))
        total = product(halves(mapped), (rh_ref[...], rl_ref[...]))
        keep_ref[...] = total[:half]
        send_ref[...] = total[half:]

    return pl.pallas_call(
        kernel,
        out_shape=(shape((half, width)),) * 2,
        in_specs=[VMEM] * (len(parts) + 4),
        out_specs=(VMEM, VMEM),
        scratch_shapes=[pltpu.VMEM((width, width), F32)],
        compiler_params=pltpu.CompilerParams(vmem_limit_bytes=16 * MIB),
        name="apply",
    )(*parts, *prepared)


def add_pieces(places, keep, received):
    piece = places.piece
    width = keep.shape[1]

    def kernel(keep_ref, received_ref, *outs):
        for slot, out in enumerate(outs):
            rows = pl.ds(slot * piece, piece)
            out[...] = keep_ref[rows, :] + received_ref[rows, :]

    return pl.pallas_call(
        kernel,
        out_shape=(shape((piece, width)),) * places.chips,
        in_specs=[VMEM, VMEM],
        out_specs=(VMEM,) * places.chips,
        compiler_params=pltpu.CompilerParams(vmem_limit_bytes=2 * MIB),
        name="add_pieces",
    )(keep, received)


def step_piece(base, pieces):
    def kernel(base_ref, *refs):
        total = refs[0][...]
        for ref in refs[1:-1]:
            total = total + ref[...]
        refs[-1][...] = base_ref[...] - STEP * total

    return pl.pallas_call(
        kernel,
        out_shape=shape(base.shape),
        in_specs=[VMEM] * (1 + len(pieces)),
        out_specs=VMEM,
        compiler_params=pltpu.CompilerParams(vmem_limit_bytes=2 * MIB),
        name="step_piece",
    )(base, *pieces)


def stack(parts):
    width = parts[0].shape[1]
    heights = [part.shape[0] for part in parts]

    def kernel(*refs):
        out = refs[-1]
        start = 0
        for ref, height in zip(refs[:-1], heights):
            out[pl.ds(start, height), :] = ref[...]
            start += height

    return pl.pallas_call(
        kernel,
        out_shape=shape((sum(heights), width)),
        in_specs=[VMEM] * len(parts),
        out_specs=VMEM,
        compiler_params=pltpu.CompilerParams(vmem_limit_bytes=2 * MIB),
        name="stack",
    )(*parts)


def spread(places, piece, with_own=True, ready=()):
    slots = [0] if with_own else []
    lines = [piece] if with_own else []
    for slot in reversed(range(1, places.rows)):
        slots.append(slot)
        lines.append(places.swap(piece, row=slot))
    mine = stack(lines)
    if ready:
        mine, *ready = lax.optimization_barrier((mine, *ready))
    chips = [mine] + [places.swap(mine, chip=slot) for slot in range(1, places.chips)]
    layout, parts = [], []
    for core_slot in range(places.cores):
        for slot, part in enumerate(chips):
            layout.append((slot, core_slot, slots, places.piece))
            parts.append(places.swap(part, core=core_slot) if core_slot else part)
    return layout, parts, ready


def reduced(places, keep, send):
    received = places.swap(send, core=1)
    own, *others = add_pieces(places, keep, received)
    return [own] + [places.swap(part, chip=slot + 1) for slot, part in enumerate(others)]


def orthogonal(places, layout, parts):
    width = parts[0].shape[1]
    slab = places.slab
    tile = 256 if width % 256 == 0 else width
    blocks = width // tile

    def kernel(*refs):
        count = len(parts)
        slab_ref, high, low, iterate, gram, poly, gram_high, gram_low, poly_high, poly_low = refs[count:]
        assemble(places, layout, refs[:count], put_in(gram))
        values = gram[...].T
        values = values * (1.0 / jnp.sqrt(jnp.sum(values * values)))
        iterate[...] = values
        high[...], low[...] = halves(values)

        def symmetric(out, left, over, finish):
            for i in range(blocks):
                rows = pl.ds(i * tile, tile)
                rest = pl.ds(i * tile, width - i * tile)
                if over == (1, 1):
                    right = (left[0][rest, :], left[1][rest, :])
                else:
                    right = (left[0][:, rest], left[1][:, rest])
                strip = finish(product((left[0][rows, :], left[1][rows, :]), right, over), rows, rest)
                out[rows, rest] = strip
                for j in range(i + 1, blocks):
                    out[pl.ds(j * tile, tile), rows] = strip[:, (j - i) * tile : (j - i + 1) * tile].T

        for repeat in range(SWEEPS):
            symmetric(gram, (high, low), (1, 1), lambda value, rows, rest: value)
            gram_high[...], gram_low[...] = halves(gram[...])
            symmetric(
                poly,
                (gram_high, gram_low),
                (1, 0),
                lambda value, rows, rest: COEF_TWO * gram[rows, rest] + COEF_THREE * value,
            )
            poly_high[...], poly_low[...] = halves(poly[...])
            right = (high[...], low[...])
            scale = math.sqrt(width) if repeat == SWEEPS - 1 else 1.0
            for i in range(blocks):
                rows = pl.ds(i * tile, tile)
                moved = product((poly_high[rows, :], poly_low[rows, :]), right)
                iterate[rows, :] = scale * (COEF_ONE * iterate[rows, :] + moved)
            high[...], low[...] = halves(iterate[...])
        gram[...] = iterate[...].T
        line = lax.axis_index("rows")
        slab_ref[...] = gram[pl.ds(pl.multiple_of(line * slab, 8), slab), :]

    square = (width, width)
    return pl.pallas_call(
        kernel,
        out_shape=(shape((slab, width)),) + (shape(square, BF16),) * 2,
        in_specs=[VMEM] * len(parts),
        out_specs=(VMEM,) * 3,
        scratch_shapes=[pltpu.VMEM(square, F32)] * 3 + [pltpu.VMEM(square, BF16)] * 4,
        compiler_params=pltpu.CompilerParams(vmem_limit_bytes=40 * MIB),
        name="orthogonal",
    )(*parts)


def environment(places, layout, parts, high, low):
    width = high.shape[0]
    slab = places.slab

    def kernel(*refs):
        count = len(parts)
        high_ref, low_ref, out_ref, block_high, block_low = refs[count:]

        def store(start, height, value):
            block_high[pl.ds(start, height), :], block_low[pl.ds(start, height), :] = halves(value)

        assemble(places, layout, refs[:count], store)
        rows = pl.ds(pl.multiple_of(lax.axis_index("rows") * slab, 16), slab)
        rotated = product((high_ref[rows, :], low_ref[rows, :]), (block_high[...], block_low[...]))
        out_ref[...] = product(halves(rotated), (high_ref[...], low_ref[...]), (1, 1))

    return pl.pallas_call(
        kernel,
        out_shape=shape((slab, width)),
        in_specs=[VMEM] * (len(parts) + 2),
        out_specs=VMEM,
        scratch_shapes=[pltpu.VMEM((width, width), BF16)] * 2,
        compiler_params=pltpu.CompilerParams(vmem_limit_bytes=16 * MIB),
        name="environment",
    )(*parts, high, low)


def combine_pieces(pieces, source_list, list_count, weight_index, weight_table):
    fan = source_list.shape[1]

    def kernel(source_ref, count_ref, index_ref, table_ref, pieces_ref, out_ref):
        for j in range(source_list.shape[0]):
            total = None
            for c in range(fan):
                weight = jnp.where(c < count_ref[j], table_ref[index_ref[j, c]], 0.0)
                term = weight * pieces_ref[source_ref[j, c]]
                total = term if total is None else total + term
            out_ref[j] = total

    return pl.pallas_call(
        kernel,
        out_shape=shape((source_list.shape[0],) + pieces.shape[1:]),
        in_specs=[SMEM] * 4 + [VMEM],
        out_specs=VMEM,
        compiler_params=pltpu.CompilerParams(vmem_limit_bytes=4 * MIB),
        name="combine",
    )(source_list, list_count, weight_index, weight_table, pieces)


def combined_slab(left, source_list, list_count, weight_index, weight_table):
    rows, width = left.shape
    owners = lax.axis_size("terms")
    if rows % (8 * owners) == 0:
        run = (rows // owners, width)
    else:
        run = (1, rows * width // owners)
    pieces = lax.all_to_all(left.reshape((owners,) + run), "terms", 0, 0, tiled=True)
    mixed = combine_pieces(pieces, source_list, list_count, weight_index, weight_table)
    return mixed, lax.all_to_all(mixed, "terms", 0, 0, tiled=True).reshape(rows, width)


def body(amplitudes, left_terms, right_terms, source_list, list_count, weight_index, weight_table):
    left, right = left_terms[0], right_terms[0]
    slab, _ = left.shape
    terms, rows = lax.axis_size("terms"), lax.axis_size("rows")
    places = Places(terms, rows, slab)

    _, combined = combined_slab(left, source_list, list_count, weight_index, weight_table)
    chip, core, line = places.here()
    every = list(range(rows))
    slabs = [(0, 0, [slot], slab) for slot in every]
    if swappable(terms, rows, slab):
        prepared = prepare(places, left, right)
        start = core * places.half + chip * places.piece
        base = lax.dynamic_slice_in_dim(amplitudes, start, places.piece, 0)
        layout, parts, prepared = spread(places, base, with_own=False, ready=prepared)
        layout, parts = [slabs[0]] + layout, [amplitudes] + parts
        for _ in range(2):
            keep, send = apply_terms(places, layout, parts, prepared)
            base = step_piece(base, reduced(places, keep, send))
            layout, parts, _ = spread(places, base)
        blocks = [combined]
        for slot in every[1:]:
            blocks.append(places.swap(combined, row=slot))
    else:
        matrix = amplitudes
        for _ in range(2):
            full = lax.all_gather(matrix, "rows", axis=0, tiled=True)
            mapped = jnp.dot(left, full, precision=HIGH)
            summed = lax.psum(jnp.dot(mapped, right, precision=HIGH), "terms")
            matrix = matrix - STEP * summed
        full = lax.all_gather(matrix, "rows", axis=0, tiled=True)
        layout = slabs
        parts = [lax.dynamic_slice_in_dim(full, (line ^ slot) * slab, slab, 0) for slot in every]
        full = lax.all_gather(combined, "rows", axis=0, tiled=True)
        blocks = [lax.dynamic_slice_in_dim(full, (line ^ slot) * slab, slab, 0) for slot in every]
    isometry, high, low = orthogonal(places, layout, parts)
    new_environment = environment(places, slabs, blocks, high, low)
    return (isometry, new_environment[None])


def swappable(terms, rows, slab):
    return terms <= 8 and terms & (terms - 1) == 0 and rows & (rows - 1) == 0 and slab % (8 * terms) == 0


def solution(mesh):
    placed = (P("rows", None), P("terms", "rows", None), P("terms", None, None), P(), P(), P(), P())

    return jax.shard_map(
        body,
        mesh=mesh,
        in_specs=placed,
        out_specs=(P("rows", None), P("terms", "rows", None)),
        check_vma=False,
    )
```

```python
import functools
import math

import jax
import jax.numpy as jnp
from jax import lax
from jax.experimental import pallas as pl
from jax.experimental.pallas import tpu as pltpu
from jax.sharding import PartitionSpec as P


SWEEPS = 3

HIGH = lax.Precision.HIGHEST
COEF_ONE = 3.4445
COEF_TWO = -4.775
COEF_THREE = 2.0315
STEP = 0.3


VMEM = pl.BlockSpec(memory_space=pltpu.VMEM)
SMEM = pl.BlockSpec(memory_space=pltpu.SMEM)
MIB = 1 << 20
BF16 = jnp.bfloat16
F32 = jnp.float32


def halves(value):
    high = value.astype(BF16)
    low = (value - high.astype(F32)).astype(BF16)
    return high, low


def product(left, right, over=(1, 0)):
    dims = (((over[0],), (over[1],)), ((), ()))
    dot = functools.partial(lax.dot_general, dimension_numbers=dims, preferred_element_type=F32)
    return dot(left[0], right[0]) + (dot(left[0], right[1]) + dot(left[1], right[0]))


def shape(dims, dtype=F32):
    return jax.ShapeDtypeStruct(dims, dtype)


class Places:
    def __init__(self, terms, rows, slab):
        self.terms, self.rows, self.slab = terms, rows, slab
        self.cores = 2
        self.chips = terms // self.cores
        self.piece = slab // terms
        self.half = slab // self.cores

    def here(self):
        term = lax.axis_index("terms")
        return term // self.cores, term % self.cores, lax.axis_index("rows")

    def swap(self, value, chip=0, core=0, row=0):
        pairs = []
        for term in range(self.terms):
            for line in range(self.rows):
                other = term ^ (chip * self.cores + core)
                pairs.append((term * self.rows + line, other * self.rows + (line ^ row)))
        return lax.ppermute(value, ("terms", "rows"), pairs)


def order_left(places, left):
    width = left.shape[1]
    piece, half = places.piece, places.half

    def kernel(left_ref, own_ref, away_ref, lh_ref, ll_ref):
        chip, core, _ = places.here()
        for side, out in enumerate((own_ref, away_ref)):
            for slot in range(places.chips):
                source = pl.multiple_of((core ^ side) * half + (chip ^ slot) * piece, 8)
                out[pl.ds(slot * piece, piece), :] = left_ref[pl.ds(source, piece), :]
            rows = pl.ds(side * half, half)
            lh_ref[rows, :], ll_ref[rows, :] = halves(out[...])

    return pl.pallas_call(
        kernel,
        out_shape=(shape((half, width)),) * 2 + (shape(left.shape, BF16),) * 2,
        in_specs=[VMEM],
        out_specs=(VMEM,) * 4,
        compiler_params=pltpu.CompilerParams(vmem_limit_bytes=4 * MIB),
        name="order_left",
    )(left)


def split_right(right):
    def kernel(right_ref, rh_ref, rl_ref):
        rh_ref[...], rl_ref[...] = halves(right_ref[...])

    return pl.pallas_call(
        kernel,
        out_shape=(shape(right.shape, BF16),) * 2,
        in_specs=[VMEM],
        out_specs=(VMEM,) * 2,
        compiler_params=pltpu.CompilerParams(vmem_limit_bytes=4 * MIB),
        name="split_right",
    )(right)


def pair_pieces(places, own, received):
    piece = places.piece
    width = own.shape[1]

    def kernel(own_ref, received_ref, *outs):
        for slot, out in enumerate(outs):
            rows = pl.ds(slot * piece, piece)
            out[pl.ds(0, piece), :] = own_ref[rows, :]
            out[pl.ds(piece, piece), :] = received_ref[rows, :]

    return pl.pallas_call(
        kernel,
        out_shape=(shape((2 * piece, width)),) * places.chips,
        in_specs=[VMEM, VMEM],
        out_specs=(VMEM,) * places.chips,
        compiler_params=pltpu.CompilerParams(vmem_limit_bytes=2 * MIB),
        name="pair_pieces",
    )(own, received)


def exchange(places, own, away):
    received = places.swap(away, core=1)
    first, *others = pair_pieces(places, own, received)
    return [first] + [places.swap(part, chip=slot + 1) for slot, part in enumerate(others)]


def by_source(places, parts, whole, stride):
    chip, core, _ = places.here()
    piece = places.piece
    for slot, part in enumerate(parts):
        for side in range(places.cores):
            start = pl.multiple_of((chip ^ slot) * stride[0] + (core ^ side) * stride[1], 8)
            whole[pl.ds(start, piece), :] = part[pl.ds(side * piece, piece), :]


def combine_exchanged(places, parts, source_list, list_count, weight_index, weight_table):
    fan = source_list.shape[1]
    width = parts[0].shape[1]
    piece, half = places.piece, places.half

    def kernel(source_ref, count_ref, index_ref, table_ref, *refs):
        *ins, own_ref, away_ref, whole = refs
        by_source(places, ins, whole, (places.cores * piece, piece))
        chip, core, _ = places.here()
        for side, out in enumerate((own_ref, away_ref)):
            for slot in range(places.chips):
                j = (chip ^ slot) * places.cores + (core ^ side)
                total = None
                for c in range(fan):
                    weight = jnp.where(c < count_ref[j], table_ref[index_ref[j, c]], 0.0)
                    start = pl.multiple_of(source_ref[j, c] * piece, 8)
                    term = weight * whole[pl.ds(start, piece), :]
                    total = term if total is None else total + term
                out[pl.ds(slot * piece, piece), :] = total

    return pl.pallas_call(
        kernel,
        out_shape=(shape((half, width)),) * 2,
        in_specs=[SMEM] * 4 + [VMEM] * len(parts),
        out_specs=(VMEM, VMEM),
        scratch_shapes=[pltpu.VMEM((places.slab, width), F32)],
        compiler_params=pltpu.CompilerParams(vmem_limit_bytes=4 * MIB),
        name="combine",
    )(source_list, list_count, weight_index, weight_table, *parts)


def place_rows(places, parts):
    width = parts[0].shape[1]

    def kernel(*refs):
        by_source(places, refs[:-1], refs[-1], (places.piece, places.half))

    return pl.pallas_call(
        kernel,
        out_shape=shape((places.slab, width)),
        in_specs=[VMEM] * len(parts),
        out_specs=VMEM,
        compiler_params=pltpu.CompilerParams(vmem_limit_bytes=2 * MIB),
        name="place_rows",
    )(*parts)


def assemble(places, layout, parts, store):
    chip, core, line = places.here()
    for (chip_slot, core_slot, row_slots, rows_each), part in zip(layout, parts):
        for index, row_slot in enumerate(row_slots):
            start = (line ^ row_slot) * places.slab
            if rows_each != places.slab:
                start = start + (core ^ core_slot) * places.half + (chip ^ chip_slot) * places.piece
            store(pl.multiple_of(start, 8), rows_each, part[pl.ds(index * rows_each, rows_each), :])


def put_in(whole):
    def store(start, height, value):
        whole[pl.ds(start, height), :] = value

    return store


def apply_terms(places, layout, parts, prepared):
    width = parts[0].shape[1]
    half = places.half

    def kernel(*refs):
        count = len(parts)
        lh_ref, ll_ref, rh_ref, rl_ref, keep_ref, send_ref, whole = refs[count:]
        assemble(places, layout, refs[:count], put_in(whole))
        mapped = product((lh_ref[...], ll_ref[...]), halves(whole[...]))
        total = product(halves(mapped), (rh_ref[...], rl_ref[...]))
        keep_ref[...] = total[:half]
        send_ref[...] = total[half:]

    return pl.pallas_call(
        kernel,
        out_shape=(shape((half, width)),) * 2,
        in_specs=[VMEM] * (len(parts) + 4),
        out_specs=(VMEM, VMEM),
        scratch_shapes=[pltpu.VMEM((width, width), F32)],
        compiler_params=pltpu.CompilerParams(vmem_limit_bytes=10 * MIB),
        name="apply",
    )(*parts, *prepared)


def add_pieces(places, keep, received):
    piece = places.piece
    width = keep.shape[1]

    def kernel(keep_ref, received_ref, *outs):
        for slot, out in enumerate(outs):
            rows = pl.ds(slot * piece, piece)
            out[...] = keep_ref[rows, :] + received_ref[rows, :]

    return pl.pallas_call(
        kernel,
        out_shape=(shape((piece, width)),) * places.chips,
        in_specs=[VMEM, VMEM],
        out_specs=(VMEM,) * places.chips,
        compiler_params=pltpu.CompilerParams(vmem_limit_bytes=2 * MIB),
        name="add_pieces",
    )(keep, received)


def step_piece(base, pieces, copies):
    def kernel(base_ref, *refs):
        ins, outs = refs[: len(pieces)], refs[len(pieces) :]
        total = ins[0][...]
        for ref in ins[1:]:
            total = total + ref[...]
        for out in outs:
            out[...] = base_ref[...] - STEP * total

    return pl.pallas_call(
        kernel,
        out_shape=(shape(base.shape),) * copies,
        in_specs=[VMEM] * (1 + len(pieces)),
        out_specs=(VMEM,) * copies,
        compiler_params=pltpu.CompilerParams(vmem_limit_bytes=2 * MIB),
        name="step_piece",
    )(base, *pieces)


def stack(parts):
    width = parts[0].shape[1]
    heights = [part.shape[0] for part in parts]

    def kernel(*refs):
        out = refs[-1]
        start = 0
        for ref, height in zip(refs[:-1], heights):
            out[pl.ds(start, height), :] = ref[...]
            start += height

    return pl.pallas_call(
        kernel,
        out_shape=shape((sum(heights), width)),
        in_specs=[VMEM] * len(parts),
        out_specs=VMEM,
        compiler_params=pltpu.CompilerParams(vmem_limit_bytes=2 * MIB),
        name="stack",
    )(*parts)


def spread(places, piece, with_own=True, ready=()):
    slots = [0] if with_own else []
    lines = [piece] if with_own else []
    for slot in reversed(range(1, places.rows)):
        slots.append(slot)
        lines.append(places.swap(piece, row=slot))
    mine = stack(lines)
    if ready:
        mine, *ready = lax.optimization_barrier((mine, *ready))
    chips = [mine] + [places.swap(mine, chip=slot) for slot in range(1, places.chips)]
    layout, parts = [], []
    for core_slot in range(places.cores):
        for slot, part in enumerate(chips):
            layout.append((slot, core_slot, slots, places.piece))
            parts.append(places.swap(part, core=core_slot) if core_slot else part)
    return layout, parts, ready


def reduced(places, keep, send):
    received = places.swap(send, core=1)
    own, *others = add_pieces(places, keep, received)
    return [own] + [places.swap(part, chip=slot + 1) for slot, part in enumerate(others)]


def orthogonal(places, layout, parts):
    width = parts[0].shape[1]
    slab = places.slab
    tile = 256 if width % 256 == 0 else width
    blocks = width // tile

    def kernel(*refs):
        count = len(parts)
        slab_ref, high, low, iterate, gram, poly, gram_high, gram_low, poly_high, poly_low = refs[count:]
        assemble(places, layout, refs[:count], put_in(gram))
        values = gram[...].T
        values = values * (1.0 / jnp.sqrt(jnp.sum(values * values)))
        iterate[...] = values
        high[...], low[...] = halves(values)

        def symmetric(out, left, over, finish):
            for i in range(blocks):
                rows = pl.ds(i * tile, tile)
                rest = pl.ds(i * tile, width - i * tile)
                if over == (1, 1):
                    right = (left[0][rest, :], left[1][rest, :])
                else:
                    right = (left[0][:, rest], left[1][:, rest])
                strip = finish(product((left[0][rows, :], left[1][rows, :]), right, over), rows, rest)
                out[rows, rest] = strip
                for j in range(i + 1, blocks):
                    out[pl.ds(j * tile, tile), rows] = strip[:, (j - i) * tile : (j - i + 1) * tile].T

        for repeat in range(SWEEPS):
            symmetric(gram, (high, low), (1, 1), lambda value, rows, rest: value)
            gram_high[...], gram_low[...] = halves(gram[...])
            symmetric(
                poly,
                (gram_high, gram_low),
                (1, 0),
                lambda value, rows, rest: COEF_TWO * gram[rows, rest] + COEF_THREE * value,
            )
            poly_high[...], poly_low[...] = halves(poly[...])
            right = (high[...], low[...])
            scale = math.sqrt(width) if repeat == SWEEPS - 1 else 1.0
            for i in range(blocks):
                rows = pl.ds(i * tile, tile)
                moved = product((poly_high[rows, :], poly_low[rows, :]), right)
                iterate[rows, :] = scale * (COEF_ONE * iterate[rows, :] + moved)
            high[...], low[...] = halves(iterate[...])
        gram[...] = iterate[...].T
        line = lax.axis_index("rows")
        slab_ref[...] = gram[pl.ds(pl.multiple_of(line * slab, 8), slab), :]

    square = (width, width)
    return pl.pallas_call(
        kernel,
        out_shape=(shape((slab, width)),) + (shape(square, BF16),) * 2,
        in_specs=[VMEM] * len(parts),
        out_specs=(VMEM,) * 3,
        scratch_shapes=[pltpu.VMEM(square, F32)] * 3 + [pltpu.VMEM(square, BF16)] * 4,
        compiler_params=pltpu.CompilerParams(vmem_limit_bytes=24 * MIB),
        name="orthogonal",
    )(*parts)


def environment(places, layout, parts, high, low):
    width = high.shape[0]
    slab = places.slab

    def kernel(*refs):
        count = len(parts)
        high_ref, low_ref, out_ref, block_high, block_low = refs[count:]

        def store(start, height, value):
            block_high[pl.ds(start, height), :], block_low[pl.ds(start, height), :] = halves(value)

        assemble(places, layout, refs[:count], store)
        rows = pl.ds(pl.multiple_of(lax.axis_index("rows") * slab, 16), slab)
        rotated = product((high_ref[rows, :], low_ref[rows, :]), (block_high[...], block_low[...]))
        out_ref[...] = product(halves(rotated), (high_ref[...], low_ref[...]), (1, 1))

    return pl.pallas_call(
        kernel,
        out_shape=shape((slab, width)),
        in_specs=[VMEM] * (len(parts) + 2),
        out_specs=VMEM,
        scratch_shapes=[pltpu.VMEM((width, width), BF16)] * 2,
        compiler_params=pltpu.CompilerParams(vmem_limit_bytes=10 * MIB),
        name="environment",
    )(*parts, high, low)


def combine_pieces(pieces, source_list, list_count, weight_index, weight_table):
    fan = source_list.shape[1]

    def kernel(source_ref, count_ref, index_ref, table_ref, pieces_ref, out_ref):
        for j in range(source_list.shape[0]):
            total = None
            for c in range(fan):
                weight = jnp.where(c < count_ref[j], table_ref[index_ref[j, c]], 0.0)
                term = weight * pieces_ref[source_ref[j, c]]
                total = term if total is None else total + term
            out_ref[j] = total

    return pl.pallas_call(
        kernel,
        out_shape=shape((source_list.shape[0],) + pieces.shape[1:]),
        in_specs=[SMEM] * 4 + [VMEM],
        out_specs=VMEM,
        compiler_params=pltpu.CompilerParams(vmem_limit_bytes=4 * MIB),
        name="combine",
    )(source_list, list_count, weight_index, weight_table, pieces)


def combined_slab(left, source_list, list_count, weight_index, weight_table):
    rows, width = left.shape
    owners = lax.axis_size("terms")
    if rows % (8 * owners) == 0:
        run = (rows // owners, width)
    else:
        run = (1, rows * width // owners)
    pieces = lax.all_to_all(left.reshape((owners,) + run), "terms", 0, 0, tiled=True)
    mixed = combine_pieces(pieces, source_list, list_count, weight_index, weight_table)
    return lax.all_to_all(mixed, "terms", 0, 0, tiled=True).reshape(rows, width)


def body(amplitudes, left_terms, right_terms, source_list, list_count, weight_index, weight_table):
    left, right = left_terms[0], right_terms[0]
    slab, _ = left.shape
    terms, rows = lax.axis_size("terms"), lax.axis_size("rows")
    places = Places(terms, rows, slab)

    lists = (source_list, list_count, weight_index, weight_table)
    chip, core, line = places.here()
    every = list(range(rows))
    slabs = [(0, 0, [slot], slab) for slot in every]
    if swappable(terms, rows, slab):
        own, away, *left_halves = order_left(places, left)
        prepared = (*left_halves, *split_right(right))
        pieces = exchange(places, own, away)
        own, away = combine_exchanged(places, pieces, *lists)
        combined = place_rows(places, exchange(places, own, away))
        start = core * places.half + chip * places.piece
        base = lax.dynamic_slice_in_dim(amplitudes, start, places.piece, 0)
        layout, parts, prepared = spread(places, base, with_own=False, ready=prepared)
        layout, parts = [slabs[0]] + layout, [amplitudes] + parts
        for name in ("f", "x"):
            keep, send = apply_terms(places, layout, parts, prepared)
            sent, *kept = step_piece(base, reduced(places, keep, send), 2 if name == "f" else 1)
            layout, parts, _ = spread(places, sent)
            base = kept[0] if kept else None
        blocks = [combined]
        for slot in every[1:]:
            blocks.append(places.swap(combined, row=slot))
    else:
        matrix = amplitudes
        for _ in range(2):
            full = lax.all_gather(matrix, "rows", axis=0, tiled=True)
            mapped = jnp.dot(left, full, precision=HIGH)
            summed = lax.psum(jnp.dot(mapped, right, precision=HIGH), "terms")
            matrix = matrix - STEP * summed
        full = lax.all_gather(matrix, "rows", axis=0, tiled=True)
        layout = slabs
        parts = [lax.dynamic_slice_in_dim(full, (line ^ slot) * slab, slab, 0) for slot in every]
        combined = combined_slab(left, *lists)
        full = lax.all_gather(combined, "rows", axis=0, tiled=True)
        blocks = [lax.dynamic_slice_in_dim(full, (line ^ slot) * slab, slab, 0) for slot in every]
    isometry, high, low = orthogonal(places, layout, parts)
    new_environment = environment(places, slabs, blocks, high, low)
    return (isometry, new_environment[None])


def swappable(terms, rows, slab):
    return terms <= 8 and terms & (terms - 1) == 0 and rows & (rows - 1) == 0 and slab % (8 * terms) == 0


def solution(mesh):
    placed = (P("rows", None), P("terms", "rows", None), P("terms", None, None), P(), P(), P(), P())

    return jax.shard_map(
        body,
        mesh=mesh,
        in_specs=placed,
        out_specs=(P("rows", None), P("terms", "rows", None)),
        check_vma=False,
    )
```

```python
import functools
import math

import jax
import jax.numpy as jnp
from jax import lax
from jax.experimental import pallas as pl
from jax.experimental.pallas import tpu as pltpu
from jax.sharding import PartitionSpec as P


SWEEPS = 3

HIGH = lax.Precision.HIGHEST
COEF_ONE = 3.4445
COEF_TWO = -4.775
COEF_THREE = 2.0315
STEP = 0.3


VMEM = pl.BlockSpec(memory_space=pltpu.VMEM)
SMEM = pl.BlockSpec(memory_space=pltpu.SMEM)
MIB = 1 << 20
BF16 = jnp.bfloat16
F32 = jnp.float32


def halves(value):
    high = value.astype(BF16)
    low = (value - high.astype(F32)).astype(BF16)
    return high, low


def product(left, right, over=(1, 0)):
    dims = (((over[0],), (over[1],)), ((), ()))
    dot = functools.partial(lax.dot_general, dimension_numbers=dims, preferred_element_type=F32)
    return dot(left[0], right[0]) + (dot(left[0], right[1]) + dot(left[1], right[0]))


def shape(dims, dtype=F32):
    return jax.ShapeDtypeStruct(dims, dtype)


class Places:
    def __init__(self, terms, rows, slab):
        self.terms, self.rows, self.slab = terms, rows, slab
        self.cores = 2
        self.chips = terms // self.cores
        self.piece = slab // terms
        self.half = slab // self.cores

    def here(self):
        term = lax.axis_index("terms")
        return term // self.cores, term % self.cores, lax.axis_index("rows")

    def swap(self, value, chip=0, core=0, row=0):
        pairs = []
        for term in range(self.terms):
            for line in range(self.rows):
                other = term ^ (chip * self.cores + core)
                pairs.append((term * self.rows + line, other * self.rows + (line ^ row)))
        return lax.ppermute(value, ("terms", "rows"), pairs)


def order_left(places, left):
    width = left.shape[1]
    piece, half = places.piece, places.half

    def kernel(left_ref, own_ref, away_ref, lh_ref, ll_ref):
        chip, core, _ = places.here()
        for side, out in enumerate((own_ref, away_ref)):
            for slot in range(places.chips):
                source = pl.multiple_of((core ^ side) * half + (chip ^ slot) * piece, 8)
                out[pl.ds(slot * piece, piece), :] = left_ref[pl.ds(source, piece), :]
            rows = pl.ds(side * half, half)
            lh_ref[rows, :], ll_ref[rows, :] = halves(out[...])

    return pl.pallas_call(
        kernel,
        out_shape=(shape((half, width)),) * 2 + (shape(left.shape, BF16),) * 2,
        in_specs=[VMEM],
        out_specs=(VMEM,) * 4,
        compiler_params=pltpu.CompilerParams(vmem_limit_bytes=4 * MIB),
        name="order_left",
    )(left)


def split_right(right, amplitudes):
    def kernel(right_ref, amplitudes_ref, rh_ref, rl_ref, copy_ref):
        rh_ref[...], rl_ref[...] = halves(right_ref[...])
        copy_ref[...] = amplitudes_ref[...]

    return pl.pallas_call(
        kernel,
        out_shape=(shape(right.shape, BF16),) * 2 + (shape(amplitudes.shape),),
        in_specs=[VMEM] * 2,
        out_specs=(VMEM,) * 3,
        compiler_params=pltpu.CompilerParams(vmem_limit_bytes=4 * MIB),
        name="split_right",
    )(right, amplitudes)


def pair_pieces(places, own, received):
    piece = places.piece
    width = own.shape[1]

    def kernel(own_ref, received_ref, *outs):
        for slot, out in enumerate(outs):
            rows = pl.ds(slot * piece, piece)
            out[pl.ds(0, piece), :] = own_ref[rows, :]
            out[pl.ds(piece, piece), :] = received_ref[rows, :]

    return pl.pallas_call(
        kernel,
        out_shape=(shape((2 * piece, width)),) * places.chips,
        in_specs=[VMEM, VMEM],
        out_specs=(VMEM,) * places.chips,
        compiler_params=pltpu.CompilerParams(vmem_limit_bytes=2 * MIB),
        name="pair_pieces",
    )(own, received)


def exchange(places, own, away):
    received = places.swap(away, core=1)
    first, *others = pair_pieces(places, own, received)
    return [first] + [places.swap(part, chip=slot + 1) for slot, part in enumerate(others)]


def by_source(places, parts, whole, stride):
    chip, core, _ = places.here()
    piece = places.piece
    for slot, part in enumerate(parts):
        for side in range(places.cores):
            start = pl.multiple_of((chip ^ slot) * stride[0] + (core ^ side) * stride[1], 8)
            whole[pl.ds(start, piece), :] = part[pl.ds(side * piece, piece), :]


def combine_exchanged(places, parts, source_list, list_count, weight_index, weight_table):
    fan = source_list.shape[1]
    source_list, weight_index = source_list.T, weight_index.T
    width = parts[0].shape[1]
    piece, half = places.piece, places.half

    def kernel(source_ref, count_ref, index_ref, table_ref, *refs):
        *ins, own_ref, away_ref, whole = refs
        by_source(places, ins, whole, (places.cores * piece, piece))
        chip, core, _ = places.here()
        for side, out in enumerate((own_ref, away_ref)):
            for slot in range(places.chips):
                j = (chip ^ slot) * places.cores + (core ^ side)
                total = None
                for c in range(fan):
                    weight = jnp.where(c < count_ref[j], table_ref[index_ref[c, j]], 0.0)
                    start = pl.multiple_of(source_ref[c, j] * piece, 8)
                    term = weight * whole[pl.ds(start, piece), :]
                    total = term if total is None else total + term
                out[pl.ds(slot * piece, piece), :] = total

    return pl.pallas_call(
        kernel,
        out_shape=(shape((half, width)),) * 2,
        in_specs=[SMEM] * 4 + [VMEM] * len(parts),
        out_specs=(VMEM, VMEM),
        scratch_shapes=[pltpu.VMEM((places.slab, width), F32)],
        compiler_params=pltpu.CompilerParams(vmem_limit_bytes=4 * MIB),
        name="combine",
    )(source_list, list_count, weight_index, weight_table, *parts)


def place_rows(places, parts):
    width = parts[0].shape[1]

    def kernel(*refs):
        by_source(places, refs[:-1], refs[-1], (places.piece, places.half))

    return pl.pallas_call(
        kernel,
        out_shape=shape((places.slab, width)),
        in_specs=[VMEM] * len(parts),
        out_specs=VMEM,
        compiler_params=pltpu.CompilerParams(vmem_limit_bytes=2 * MIB),
        name="place_rows",
    )(*parts)


def assemble(places, layout, parts, store):
    chip, core, line = places.here()
    for (core_slot, blocks), part in zip(layout, parts):
        for index, (chip_slot, row_slot) in enumerate(blocks):
            start, height = (line ^ row_slot) * places.slab, places.slab
            if chip_slot is not None:
                start = start + (core ^ core_slot) * places.half + (chip ^ chip_slot) * places.piece
                height = places.piece
            store(pl.multiple_of(start, 8), height, part[pl.ds(index * height, height), :])


def put_in(whole):
    def store(start, height, value):
        whole[pl.ds(start, height), :] = value

    return store


def apply_terms(places, layout, parts, prepared):
    width = parts[0].shape[1]
    half = places.half

    def kernel(*refs):
        count = len(parts)
        lh_ref, ll_ref, rh_ref, rl_ref, keep_ref, send_ref, whole = refs[count:]
        assemble(places, layout, refs[:count], put_in(whole))
        mapped = product((lh_ref[...], ll_ref[...]), halves(whole[...]))
        total = product(halves(mapped), (rh_ref[...], rl_ref[...]))
        keep_ref[...] = total[:half]
        send_ref[...] = total[half:]

    return pl.pallas_call(
        kernel,
        out_shape=(shape((half, width)),) * 2,
        in_specs=[VMEM] * (len(parts) + 4),
        out_specs=(VMEM, VMEM),
        scratch_shapes=[pltpu.VMEM((width, width), F32)],
        compiler_params=pltpu.CompilerParams(vmem_limit_bytes=10 * MIB),
        name="apply",
    )(*parts, *prepared)


def add_pieces(places, keep, received):
    piece = places.piece
    width = keep.shape[1]

    def kernel(keep_ref, received_ref, *outs):
        for slot, out in enumerate(outs):
            rows = pl.ds(slot * piece, piece)
            out[...] = keep_ref[rows, :] + received_ref[rows, :]

    return pl.pallas_call(
        kernel,
        out_shape=(shape((piece, width)),) * places.chips,
        in_specs=[VMEM, VMEM],
        out_specs=(VMEM,) * places.chips,
        compiler_params=pltpu.CompilerParams(vmem_limit_bytes=2 * MIB),
        name="add_pieces",
    )(keep, received)


def step_piece(base, pieces, copies):
    def kernel(base_ref, *refs):
        ins, outs = refs[: len(pieces)], refs[len(pieces) :]
        total = ins[0][...]
        for ref in ins[1:]:
            total = total + ref[...]
        for out in outs:
            out[...] = base_ref[...] - STEP * total

    return pl.pallas_call(
        kernel,
        out_shape=(shape(base.shape),) * copies,
        in_specs=[VMEM] * (1 + len(pieces)),
        out_specs=(VMEM,) * copies,
        compiler_params=pltpu.CompilerParams(vmem_limit_bytes=2 * MIB),
        name="step_piece",
    )(base, *pieces)


def stack(parts):
    width = parts[0].shape[1]
    heights = [part.shape[0] for part in parts]

    def kernel(*refs):
        out = refs[-1]
        start = 0
        for ref, height in zip(refs[:-1], heights):
            out[pl.ds(start, height), :] = ref[...]
            start += height

    return pl.pallas_call(
        kernel,
        out_shape=shape((sum(heights), width)),
        in_specs=[VMEM] * len(parts),
        out_specs=VMEM,
        compiler_params=pltpu.CompilerParams(vmem_limit_bytes=2 * MIB),
        name="stack",
    )(*parts)


def spread(places, piece, with_own=True, ready=()):
    chips = range(1, places.chips)
    slots = list(reversed(range(1, places.rows)))
    layout, parts = [], []

    def both_cores(blocks, part):
        other = places.swap(part, core=1)
        layout.extend([(0, blocks), (1, blocks)])
        parts.extend([part, other])

    lines = [places.swap(piece, row=slot) for slot in slots]
    if with_own:
        own = [piece] + [places.swap(piece, chip=slot) for slot in chips]
    mine = stack(lines)
    if ready:
        mine, *ready = lax.optimization_barrier((mine, *ready))
    gathered = [mine] + [places.swap(mine, chip=slot) for slot in chips]
    if with_own:
        both_cores([(slot, 0) for slot in range(places.chips)], stack(own))
    for chip_slot, part in enumerate(gathered):
        both_cores([(chip_slot, slot) for slot in slots], part)
    return layout, parts, ready


def reduced(places, keep, send):
    received = places.swap(send, core=1)
    own, *others = add_pieces(places, keep, received)
    return [own] + [places.swap(part, chip=slot + 1) for slot, part in enumerate(others)]


def orthogonal(places, layout, parts):
    width = parts[0].shape[1]
    slab = places.slab
    tile = 256 if width % 256 == 0 else width
    blocks = width // tile

    def kernel(*refs):
        count = len(parts)
        slab_ref, high, low, iterate, gram, gram_high, gram_low, poly_high, poly_low, *spare = refs[count:]
        pairs = (spare[:2], spare[2:])
        assemble(places, layout, refs[:count], put_in(gram))
        values = gram[...].T
        values = values * (1.0 / jnp.sqrt(jnp.sum(values * values)))
        iterate[...] = values
        spare[0][...], spare[1][...] = halves(values)

        def symmetric(left, over, finish, out_high, out_low):
            for i in range(blocks):
                rows = pl.ds(i * tile, tile)
                rest = pl.ds(i * tile, width - i * tile)
                if over == (1, 1):
                    right = (left[0][rest, :], left[1][rest, :])
                else:
                    right = (left[0][:, rest], left[1][:, rest])
                strip = finish(product((left[0][rows, :], left[1][rows, :]), right, over), rows, rest)
                out_high[rows, rest], out_low[rows, rest] = halves(strip)
                for j in range(i + 1, blocks):
                    below = pl.ds(j * tile, tile)
                    mirrored = strip[:, (j - i) * tile : (j - i + 1) * tile].T
                    out_high[below, rows], out_low[below, rows] = halves(mirrored)

        def keep_gram(value, rows, rest):
            gram[rows, rest] = value
            return value

        def polynomial(value, rows, rest):
            return COEF_TWO * gram[rows, rest] + COEF_THREE * value

        for repeat in range(SWEEPS):
            here, there = pairs[repeat % 2], pairs[(repeat + 1) % 2]
            symmetric(here, (1, 1), keep_gram, gram_high, gram_low)
            symmetric((gram_high, gram_low), (1, 0), polynomial, poly_high, poly_low)
            last = repeat == SWEEPS - 1
            scale = math.sqrt(width) if last else 1.0
            there = (high, low) if last else there
            for i in range(blocks):
                rows = pl.ds(i * tile, tile)
                moved = product((poly_high[rows, :], poly_low[rows, :]), (here[0][...], here[1][...]))
                values = scale * (COEF_ONE * iterate[rows, :] + moved)
                iterate[rows, :] = values
                there[0][rows, :], there[1][rows, :] = halves(values)
        gram[...] = iterate[...].T
        line = lax.axis_index("rows")
        slab_ref[...] = gram[pl.ds(pl.multiple_of(line * slab, 8), slab), :]

    square = (width, width)
    return pl.pallas_call(
        kernel,
        out_shape=(shape((slab, width)),) + (shape(square, BF16),) * 2,
        in_specs=[VMEM] * len(parts),
        out_specs=(VMEM,) * 3,
        scratch_shapes=[pltpu.VMEM(square, F32)] * 2 + [pltpu.VMEM(square, BF16)] * 8,
        compiler_params=pltpu.CompilerParams(vmem_limit_bytes=24 * MIB),
        name="orthogonal",
    )(*parts)


def environment(places, layout, parts, high, low):
    width = high.shape[0]
    slab = places.slab

    def kernel(*refs):
        count = len(parts)
        high_ref, low_ref, out_ref, block_high, block_low = refs[count:]

        def store(start, height, value):
            block_high[pl.ds(start, height), :], block_low[pl.ds(start, height), :] = halves(value)

        assemble(places, layout, refs[:count], store)
        rows = pl.ds(pl.multiple_of(lax.axis_index("rows") * slab, 16), slab)
        rotated = product((high_ref[rows, :], low_ref[rows, :]), (block_high[...], block_low[...]))
        out_ref[...] = product(halves(rotated), (high_ref[...], low_ref[...]), (1, 1))

    return pl.pallas_call(
        kernel,
        out_shape=shape((slab, width)),
        in_specs=[VMEM] * (len(parts) + 2),
        out_specs=VMEM,
        scratch_shapes=[pltpu.VMEM((width, width), BF16)] * 2,
        compiler_params=pltpu.CompilerParams(vmem_limit_bytes=10 * MIB),
        name="environment",
    )(*parts, high, low)


def combine_pieces(pieces, source_list, list_count, weight_index, weight_table):
    fan = source_list.shape[1]

    def kernel(source_ref, count_ref, index_ref, table_ref, pieces_ref, out_ref):
        for j in range(source_list.shape[0]):
            total = None
            for c in range(fan):
                weight = jnp.where(c < count_ref[j], table_ref[index_ref[j, c]], 0.0)
                term = weight * pieces_ref[source_ref[j, c]]
                total = term if total is None else total + term
            out_ref[j] = total

    return pl.pallas_call(
        kernel,
        out_shape=shape((source_list.shape[0],) + pieces.shape[1:]),
        in_specs=[SMEM] * 4 + [VMEM],
        out_specs=VMEM,
        compiler_params=pltpu.CompilerParams(vmem_limit_bytes=4 * MIB),
        name="combine",
    )(source_list, list_count, weight_index, weight_table, pieces)


def combined_slab(left, source_list, list_count, weight_index, weight_table):
    rows, width = left.shape
    owners = lax.axis_size("terms")
    if rows % (8 * owners) == 0:
        run = (rows // owners, width)
    else:
        run = (1, rows * width // owners)
    pieces = lax.all_to_all(left.reshape((owners,) + run), "terms", 0, 0, tiled=True)
    mixed = combine_pieces(pieces, source_list, list_count, weight_index, weight_table)
    return lax.all_to_all(mixed, "terms", 0, 0, tiled=True).reshape(rows, width)


def body(amplitudes, left_terms, right_terms, source_list, list_count, weight_index, weight_table):
    left, right = left_terms[0], right_terms[0]
    slab, _ = left.shape
    terms, rows = lax.axis_size("terms"), lax.axis_size("rows")
    places = Places(terms, rows, slab)

    lists = (source_list, list_count, weight_index, weight_table)
    chip, core, line = places.here()
    every = list(range(rows))
    slabs = [(0, [(None, slot)]) for slot in every]
    if swappable(terms, rows, slab):
        own, away, *left_halves = order_left(places, left)
        prepared = (*left_halves, *split_right(right, amplitudes))
        pieces = exchange(places, own, away)
        own, away = combine_exchanged(places, pieces, *lists)
        combined = place_rows(places, exchange(places, own, away))
        start = core * places.half + chip * places.piece
        base = lax.dynamic_slice_in_dim(amplitudes, start, places.piece, 0)
        layout, parts, prepared = spread(places, base, with_own=False, ready=prepared)
        *prepared, amplitudes = prepared
        layout, parts = [slabs[0]] + layout, [amplitudes] + parts
        for name in ("f", "x"):
            keep, send = apply_terms(places, layout, parts, prepared)
            pieces = reduced(places, keep, send)
            sent, *kept = step_piece(base, pieces, 2 if name == "f" else 1)
            layout, parts, _ = spread(places, sent)
            base = kept[0] if kept else None
        blocks = [combined]
        for slot in every[1:]:
            blocks.append(places.swap(combined, row=slot))
    else:
        matrix = amplitudes
        for _ in range(2):
            full = lax.all_gather(matrix, "rows", axis=0, tiled=True)
            mapped = jnp.dot(left, full, precision=HIGH)
            summed = lax.psum(jnp.dot(mapped, right, precision=HIGH), "terms")
            matrix = matrix - STEP * summed
        full = lax.all_gather(matrix, "rows", axis=0, tiled=True)
        layout = slabs
        parts = [lax.dynamic_slice_in_dim(full, (line ^ slot) * slab, slab, 0) for slot in every]
        combined = combined_slab(left, *lists)
        full = lax.all_gather(combined, "rows", axis=0, tiled=True)
        blocks = [lax.dynamic_slice_in_dim(full, (line ^ slot) * slab, slab, 0) for slot in every]
    isometry, high, low = orthogonal(places, layout, parts)
    new_environment = environment(places, slabs, blocks, high, low)
    return (isometry, new_environment[None])


def swappable(terms, rows, slab):
    return terms <= 8 and terms & (terms - 1) == 0 and rows & (rows - 1) == 0 and slab % (8 * terms) == 0


def solution(mesh):
    placed = (P("rows", None), P("terms", "rows", None), P("terms", None, None), P(), P(), P(), P())

    return jax.shard_map(
        body,
        mesh=mesh,
        in_specs=placed,
        out_specs=(P("rows", None), P("terms", "rows", None)),
        check_vma=False,
    )
```

```python
import functools
import math

import jax
import jax.numpy as jnp
from jax import lax
from jax.experimental import pallas as pl
from jax.experimental.pallas import tpu as pltpu
from jax.sharding import PartitionSpec as P


SWEEPS = 3

HIGH = lax.Precision.HIGHEST
COEF_ONE = 3.4445
COEF_TWO = -4.775
COEF_THREE = 2.0315
STEP = 0.3


VMEM = pl.BlockSpec(memory_space=pltpu.VMEM)
SMEM = pl.BlockSpec(memory_space=pltpu.SMEM)
MIB = 1 << 20
BF16 = jnp.bfloat16
F32 = jnp.float32


def halves(value):
    high = value.astype(BF16)
    low = (value - high.astype(F32)).astype(BF16)
    return high, low


def product(left, right, over=(1, 0)):
    dims = (((over[0],), (over[1],)), ((), ()))
    dot = functools.partial(lax.dot_general, dimension_numbers=dims, preferred_element_type=F32)
    count = left[0].shape[0]
    both = dot(jnp.concatenate(left, axis=0), right[0])
    return both[:count] + (both[count:] + dot(left[0], right[1]))


def shape(dims, dtype=F32):
    return jax.ShapeDtypeStruct(dims, dtype)


class Places:
    def __init__(self, terms, rows, slab):
        self.terms, self.rows, self.slab = terms, rows, slab
        self.cores = 2
        self.chips = terms // self.cores
        self.piece = slab // terms
        self.half = slab // self.cores

    def here(self):
        term = lax.axis_index("terms")
        return term // self.cores, term % self.cores, lax.axis_index("rows")

    def swap(self, value, chip=0, core=0, row=0):
        pairs = []
        for term in range(self.terms):
            for line in range(self.rows):
                other = term ^ (chip * self.cores + core)
                pairs.append((term * self.rows + line, other * self.rows + (line ^ row)))
        return lax.ppermute(value, ("terms", "rows"), pairs)


def order_left(places, left):
    width = left.shape[1]
    piece, half = places.piece, places.half

    def kernel(left_ref, own_ref, away_ref, lh_ref, ll_ref):
        chip, core, _ = places.here()
        for side, out in enumerate((own_ref, away_ref)):
            for slot in range(places.chips):
                source = pl.multiple_of((core ^ side) * half + (chip ^ slot) * piece, 8)
                out[pl.ds(slot * piece, piece), :] = left_ref[pl.ds(source, piece), :]
            rows = pl.ds(side * half, half)
            lh_ref[rows, :], ll_ref[rows, :] = halves(out[...])

    return pl.pallas_call(
        kernel,
        out_shape=(shape((half, width)),) * 2 + (shape(left.shape, BF16),) * 2,
        in_specs=[VMEM],
        out_specs=(VMEM,) * 4,
        compiler_params=pltpu.CompilerParams(vmem_limit_bytes=4 * MIB),
        name="order_left",
    )(left)


def split_right(places, right, amplitudes):
    def kernel(right_ref, amplitudes_ref, rh_ref, rl_ref, copy_ref, base_ref):
        rh_ref[...], rl_ref[...] = halves(right_ref[...])
        copy_ref[...] = amplitudes_ref[...]
        chip, core, _ = places.here()
        start = pl.multiple_of(core * places.half + chip * places.piece, 8)
        base_ref[...] = amplitudes_ref[pl.ds(start, places.piece), :]

    return pl.pallas_call(
        kernel,
        out_shape=(shape(right.shape, BF16),) * 2
        + (shape(amplitudes.shape), shape((places.piece, right.shape[1]))),
        in_specs=[VMEM] * 2,
        out_specs=(VMEM,) * 4,
        compiler_params=pltpu.CompilerParams(vmem_limit_bytes=4 * MIB),
        name="split_right",
    )(right, amplitudes)


def pair_pieces(places, own, received):
    piece = places.piece
    width = own.shape[1]

    def kernel(own_ref, received_ref, *outs):
        for slot, out in enumerate(outs):
            rows = pl.ds(slot * piece, piece)
            out[pl.ds(0, piece), :] = own_ref[rows, :]
            out[pl.ds(piece, piece), :] = received_ref[rows, :]

    return pl.pallas_call(
        kernel,
        out_shape=(shape((2 * piece, width)),) * places.chips,
        in_specs=[VMEM, VMEM],
        out_specs=(VMEM,) * places.chips,
        compiler_params=pltpu.CompilerParams(vmem_limit_bytes=2 * MIB),
        name="pair_pieces",
    )(own, received)


def exchange(places, own, away):
    received = places.swap(away, core=1)
    first, *others = pair_pieces(places, own, received)
    return [first] + [places.swap(part, chip=slot + 1) for slot, part in enumerate(others)]


def by_source(places, parts, whole, stride):
    chip, core, _ = places.here()
    piece = places.piece
    for slot, part in enumerate(parts):
        for side in range(places.cores):
            start = pl.multiple_of((chip ^ slot) * stride[0] + (core ^ side) * stride[1], 8)
            whole[pl.ds(start, piece), :] = part[pl.ds(side * piece, piece), :]


def combine_exchanged(places, parts, source_list, list_count, weight_index, weight_table):
    fan = source_list.shape[1]
    source_list, weight_index = source_list.T, weight_index.T
    width = parts[0].shape[1]
    piece, half = places.piece, places.half

    def kernel(source_ref, count_ref, index_ref, table_ref, *refs):
        *ins, own_ref, away_ref, whole = refs
        by_source(places, ins, whole, (places.cores * piece, piece))
        chip, core, _ = places.here()
        for side, out in enumerate((own_ref, away_ref)):
            for slot in range(places.chips):
                j = (chip ^ slot) * places.cores + (core ^ side)
                total = None
                for c in range(fan):
                    weight = jnp.where(c < count_ref[j], table_ref[index_ref[c, j]], 0.0)
                    start = pl.multiple_of(source_ref[c, j] * piece, 8)
                    term = weight * whole[pl.ds(start, piece), :]
                    total = term if total is None else total + term
                out[pl.ds(slot * piece, piece), :] = total

    return pl.pallas_call(
        kernel,
        out_shape=(shape((half, width)),) * 2,
        in_specs=[SMEM] * 4 + [VMEM] * len(parts),
        out_specs=(VMEM, VMEM),
        scratch_shapes=[pltpu.VMEM((places.slab, width), F32)],
        compiler_params=pltpu.CompilerParams(vmem_limit_bytes=4 * MIB),
        name="combine",
    )(source_list, list_count, weight_index, weight_table, *parts)


def place_rows(places, parts):
    width = parts[0].shape[1]

    def kernel(*refs):
        by_source(places, refs[:-1], refs[-1], (places.piece, places.half))

    return pl.pallas_call(
        kernel,
        out_shape=shape((places.slab, width)),
        in_specs=[VMEM] * len(parts),
        out_specs=VMEM,
        compiler_params=pltpu.CompilerParams(vmem_limit_bytes=2 * MIB),
        name="place_rows",
    )(*parts)


def assemble(places, layout, parts, store):
    chip, core, line = places.here()
    for (core_slot, blocks), part in zip(layout, parts):
        first = 0
        for row_slot, height, place in blocks:
            start = (line ^ row_slot) * places.slab + place(chip, core ^ core_slot)
            store(pl.multiple_of(start, 8), height, part[pl.ds(first, height), :])
            first += height


def put_in(whole):
    def store(start, height, value):
        whole[pl.ds(start, height), :] = value

    return store


def apply_terms(places, layout, parts, prepared):
    width = parts[0].shape[1]
    half = places.half

    def kernel(*refs):
        count = len(parts)
        lh_ref, ll_ref, rh_ref, rl_ref, keep_ref, send_ref, whole = refs[count:]
        assemble(places, layout, refs[:count], put_in(whole))
        mapped = product((lh_ref[...], ll_ref[...]), halves(whole[...]))
        total = product(halves(mapped), (rh_ref[...], rl_ref[...]))
        keep_ref[...] = total[:half]
        send_ref[...] = total[half:]

    return pl.pallas_call(
        kernel,
        out_shape=(shape((half, width)),) * 2,
        in_specs=[VMEM] * (len(parts) + 4),
        out_specs=(VMEM, VMEM),
        scratch_shapes=[pltpu.VMEM((width, width), F32)],
        compiler_params=pltpu.CompilerParams(vmem_limit_bytes=10 * MIB),
        name="apply",
    )(*parts, *prepared)


def add_pieces(places, keep, received):
    piece = places.piece
    width = keep.shape[1]

    def kernel(keep_ref, received_ref, *outs):
        for slot, out in enumerate(outs):
            rows = pl.ds(slot * piece, piece)
            out[...] = keep_ref[rows, :] + received_ref[rows, :]

    return pl.pallas_call(
        kernel,
        out_shape=(shape((piece, width)),) * places.chips,
        in_specs=[VMEM, VMEM],
        out_specs=(VMEM,) * places.chips,
        compiler_params=pltpu.CompilerParams(vmem_limit_bytes=2 * MIB),
        name="add_pieces",
    )(keep, received)


def step_piece(base, pieces, copies):
    def kernel(base_ref, *refs):
        ins, outs = refs[: len(pieces)], refs[len(pieces) :]
        total = ins[0][...]
        for ref in ins[1:]:
            total = total + ref[...]
        for out in outs:
            out[...] = base_ref[...] - STEP * total

    return pl.pallas_call(
        kernel,
        out_shape=(shape(base.shape),) * copies,
        in_specs=[VMEM] * (1 + len(pieces)),
        out_specs=(VMEM,) * copies,
        compiler_params=pltpu.CompilerParams(vmem_limit_bytes=2 * MIB),
        name="step_piece",
    )(base, *pieces)


def stack(parts):
    width = parts[0].shape[1]
    heights = [part.shape[0] for part in parts]

    def kernel(*refs):
        out = refs[-1]
        start = 0
        for ref, height in zip(refs[:-1], heights):
            out[pl.ds(start, height), :] = ref[...]
            start += height

    return pl.pallas_call(
        kernel,
        out_shape=shape((sum(heights), width)),
        in_specs=[VMEM] * len(parts),
        out_specs=VMEM,
        compiler_params=pltpu.CompilerParams(vmem_limit_bytes=2 * MIB),
        name="stack",
    )(*parts)


def to_both_cores(places, layout, parts, blocks, part):
    other = places.swap(part, core=1)
    layout.extend([(0, blocks), (1, blocks)])
    parts.extend([part, other])


def spread(places, piece):
    chips = range(1, places.chips)
    slots = list(reversed(range(1, places.rows)))
    layout, parts = [], []

    def blocks(pairs):
        def place(slot):
            return lambda chip, core: core * places.half + (chip ^ slot) * places.piece

        return [(row_slot, places.piece, place(chip_slot)) for chip_slot, row_slot in pairs]

    lines = [places.swap(piece, row=slot) for slot in slots]
    own = [piece] + [places.swap(piece, chip=slot) for slot in chips]
    mine = stack(lines)
    gathered = [mine] + [places.swap(mine, chip=slot) for slot in chips]
    own = stack(own)
    to_both_cores(places, layout, parts, blocks([(slot, 0) for slot in range(places.chips)]), own)
    for chip_slot, part in enumerate(gathered):
        to_both_cores(places, layout, parts, blocks([(chip_slot, slot) for slot in slots]), part)
    return layout, parts


def spread_slabs(places, slab, ready):
    part_rows, piece = 2 * places.piece, places.piece
    slots = list(reversed(range(1, places.rows)))
    chip, core, _ = places.here()

    def parity(chip):
        return (chip & 1) ^ (chip >> 1)

    def place(turn, extra):
        return lambda chip, core: core * places.half + (parity(chip) ^ turn) * part_rows + extra

    start = core * places.half + parity(chip) * part_rows
    sent = lax.dynamic_slice_in_dim(slab, start, part_rows, 0)
    lines = [places.swap(sent, row=slot) for slot in slots]
    firsts, rests = stack_halves(lines)
    firsts, rests, *ready = lax.optimization_barrier((firsts, rests, *ready))
    layout, parts = [], []
    others = [places.swap(firsts, chip=1), places.swap(rests, chip=2)]
    for turn, extra, part in ((0, 0, firsts), (0, piece, rests), (1, 0, others[0]), (1, piece, others[1])):
        blocks = [(slot, piece, place(turn, extra)) for slot in slots]
        to_both_cores(places, layout, parts, blocks, part)
    return layout, parts, ready


def stack_halves(parts):
    width = parts[0].shape[1]
    height = parts[0].shape[0] // 2

    def kernel(*refs):
        for side, out in enumerate(refs[-2:]):
            for index, ref in enumerate(refs[:-2]):
                out[pl.ds(index * height, height), :] = ref[pl.ds(side * height, height), :]

    return pl.pallas_call(
        kernel,
        out_shape=(shape((height * len(parts), width)),) * 2,
        in_specs=[VMEM] * len(parts),
        out_specs=(VMEM,) * 2,
        compiler_params=pltpu.CompilerParams(vmem_limit_bytes=2 * MIB),
        name="stack_halves",
    )(*parts)


def reduced(places, keep, send):
    received = places.swap(send, core=1)
    own, *others = add_pieces(places, keep, received)
    return [own] + [places.swap(part, chip=slot + 1) for slot, part in enumerate(others)]


def orthogonal(places, layout, parts):
    width = parts[0].shape[1]
    slab = places.slab
    tile = 256 if width % 256 == 0 else width
    blocks = width // tile

    def kernel(*refs):
        count = len(parts)
        slab_ref, high, low, mine_high, mine_low = refs[count : count + 5]
        iterate, gram, gram_high, gram_low, poly_high, poly_low, *spare = refs[count + 5 :]
        pairs = (spare[:2], spare[2:])
        assemble(places, layout, refs[:count], put_in(gram))
        squares = jnp.zeros((8, width), F32)
        for i in range(width // 8):
            some = gram[pl.ds(8 * i, 8), :]
            squares = squares + some * some
        values = gram[...].T * (1.0 / jnp.sqrt(jnp.sum(squares)))
        iterate[...] = values
        spare[0][...], spare[1][...] = halves(values)

        def symmetric(left, over, finish, out_high, out_low):
            for i in range(blocks):
                rows = pl.ds(i * tile, tile)
                rest = pl.ds(i * tile, width - i * tile)
                if over == (1, 1):
                    right = (left[0][rest, :], left[1][rest, :])
                else:
                    right = (left[0][:, rest], left[1][:, rest])
                strip = finish(product((left[0][rows, :], left[1][rows, :]), right, over), rows, rest)
                out_high[rows, rest], out_low[rows, rest] = halves(strip)
                for j in range(i + 1, blocks):
                    below = pl.ds(j * tile, tile)
                    mirrored = strip[:, (j - i) * tile : (j - i + 1) * tile].T
                    out_high[below, rows], out_low[below, rows] = halves(mirrored)

        def keep_gram(value, rows, rest):
            gram[rows, rest] = value
            return value

        def polynomial(value, rows, rest):
            return COEF_TWO * gram[rows, rest] + COEF_THREE * value

        for repeat in range(SWEEPS):
            here, there = pairs[repeat % 2], pairs[(repeat + 1) % 2]
            symmetric(here, (1, 1), keep_gram, gram_high, gram_low)
            symmetric((gram_high, gram_low), (1, 0), polynomial, poly_high, poly_low)
            for i in range(blocks):
                rows = pl.ds(i * tile, tile)
                moved = product((poly_high[rows, :], poly_low[rows, :]), (here[0][...], here[1][...]))
                values = COEF_ONE * iterate[rows, :] + moved
                if repeat < SWEEPS - 1:
                    iterate[rows, :] = values
                    there[0][rows, :], there[1][rows, :] = halves(values)
                else:
                    values = math.sqrt(width) * values
                    iterate[rows, :] = values
                    upright = values.T
                    gram[:, rows] = upright
                    high[:, rows], low[:, rows] = halves(upright)
        mine = pl.ds(pl.multiple_of(lax.axis_index("rows") * slab, 8), slab)
        slab_ref[...] = gram[mine, :]
        mine_high[...], mine_low[...] = halves(iterate[mine, :])

    square = (width, width)
    return pl.pallas_call(
        kernel,
        out_shape=(shape((slab, width)),) + (shape(square, BF16),) * 2 + (shape((slab, width), BF16),) * 2,
        in_specs=[VMEM] * len(parts),
        out_specs=(VMEM,) * 5,
        scratch_shapes=[pltpu.VMEM(square, F32)] * 2 + [pltpu.VMEM(square, BF16)] * 8,
        compiler_params=pltpu.CompilerParams(vmem_limit_bytes=24 * MIB),
        name="orthogonal",
    )(*parts)


def environment(places, layout, parts, high, low, mine_high, mine_low):
    width = high.shape[0]
    slab = places.slab

    def kernel(*refs):
        count = len(parts)
        high_ref, low_ref, mh_ref, ml_ref, out_ref, block_high, block_low = refs[count:]

        def store(start, height, value):
            block_high[pl.ds(start, height), :], block_low[pl.ds(start, height), :] = halves(value)

        assemble(places, layout, refs[:count], store)
        rotated = product((mh_ref[...], ml_ref[...]), (block_high[...], block_low[...]))
        out_ref[...] = product(halves(rotated), (high_ref[...], low_ref[...]))

    return pl.pallas_call(
        kernel,
        out_shape=shape((slab, width)),
        in_specs=[VMEM] * (len(parts) + 4),
        out_specs=VMEM,
        scratch_shapes=[pltpu.VMEM((width, width), BF16)] * 2,
        compiler_params=pltpu.CompilerParams(vmem_limit_bytes=10 * MIB),
        name="environment",
    )(*parts, high, low, mine_high, mine_low)


def combine_pieces(pieces, source_list, list_count, weight_index, weight_table):
    fan = source_list.shape[1]

    def kernel(source_ref, count_ref, index_ref, table_ref, pieces_ref, out_ref):
        for j in range(source_list.shape[0]):
            total = None
            for c in range(fan):
                weight = jnp.where(c < count_ref[j], table_ref[index_ref[j, c]], 0.0)
                term = weight * pieces_ref[source_ref[j, c]]
                total = term if total is None else total + term
            out_ref[j] = total

    return pl.pallas_call(
        kernel,
        out_shape=shape((source_list.shape[0],) + pieces.shape[1:]),
        in_specs=[SMEM] * 4 + [VMEM],
        out_specs=VMEM,
        compiler_params=pltpu.CompilerParams(vmem_limit_bytes=4 * MIB),
        name="combine",
    )(source_list, list_count, weight_index, weight_table, pieces)


def combined_slab(left, source_list, list_count, weight_index, weight_table):
    rows, width = left.shape
    owners = lax.axis_size("terms")
    if rows % (8 * owners) == 0:
        run = (rows // owners, width)
    else:
        run = (1, rows * width // owners)
    pieces = lax.all_to_all(left.reshape((owners,) + run), "terms", 0, 0, tiled=True)
    mixed = combine_pieces(pieces, source_list, list_count, weight_index, weight_table)
    return lax.all_to_all(mixed, "terms", 0, 0, tiled=True).reshape(rows, width)


def body(amplitudes, left_terms, right_terms, source_list, list_count, weight_index, weight_table):
    left, right = left_terms[0], right_terms[0]
    slab, _ = left.shape
    terms, rows = lax.axis_size("terms"), lax.axis_size("rows")
    places = Places(terms, rows, slab)

    lists = (source_list, list_count, weight_index, weight_table)
    _, _, line = places.here()
    every = list(range(rows))
    slabs = [(0, [(slot, slab, lambda chip, core: 0)]) for slot in every]
    if swappable(terms, rows, slab):
        own, away, *left_halves = order_left(places, left)
        prepared = (*left_halves, *split_right(places, right, amplitudes))
        pieces = exchange(places, own, away)
        own, away = combine_exchanged(places, pieces, *lists)
        combined = place_rows(places, exchange(places, own, away))
        layout, parts, prepared = spread_slabs(places, amplitudes, prepared)
        *prepared, amplitudes, base = prepared
        layout, parts = [slabs[0]] + layout, [amplitudes] + parts
        for name in ("f", "x"):
            keep, send = apply_terms(places, layout, parts, prepared)
            pieces = reduced(places, keep, send)
            sent, *kept = step_piece(base, pieces, 2 if name == "f" else 1)
            layout, parts = spread(places, sent)
            base = kept[0] if kept else None
        blocks = [combined]
        for slot in every[1:]:
            blocks.append(places.swap(combined, row=slot))
    else:
        matrix = amplitudes
        for _ in range(2):
            full = lax.all_gather(matrix, "rows", axis=0, tiled=True)
            mapped = jnp.dot(left, full, precision=HIGH)
            summed = lax.psum(jnp.dot(mapped, right, precision=HIGH), "terms")
            matrix = matrix - STEP * summed
        full = lax.all_gather(matrix, "rows", axis=0, tiled=True)
        layout = slabs
        parts = [lax.dynamic_slice_in_dim(full, (line ^ slot) * slab, slab, 0) for slot in every]
        combined = combined_slab(left, *lists)
        full = lax.all_gather(combined, "rows", axis=0, tiled=True)
        blocks = [lax.dynamic_slice_in_dim(full, (line ^ slot) * slab, slab, 0) for slot in every]
    isometry, *turned = orthogonal(places, layout, parts)
    new_environment = environment(places, slabs, blocks, *turned)
    return (isometry, new_environment[None])


def swappable(terms, rows, slab):
    return terms == 8 and rows & (rows - 1) == 0 and slab % (8 * terms) == 0


def solution(mesh):
    placed = (P("rows", None), P("terms", "rows", None), P("terms", None, None), P(), P(), P(), P())

    return jax.shard_map(
        body,
        mesh=mesh,
        in_specs=placed,
        out_specs=(P("rows", None), P("terms", "rows", None)),
        check_vma=False,
    )
```

```python
import functools
import math

import jax
import jax.numpy as jnp
from jax import lax
from jax.experimental import pallas as pl
from jax.experimental.pallas import tpu as pltpu
from jax.sharding import PartitionSpec as P


SWEEPS = 3

HIGH = lax.Precision.HIGHEST
COEF_ONE = 3.4445
COEF_TWO = -4.775
COEF_THREE = 2.0315
STEP = 0.3


VMEM = pl.BlockSpec(memory_space=pltpu.VMEM)
SMEM = pl.BlockSpec(memory_space=pltpu.SMEM)
MIB = 1 << 20
BF16 = jnp.bfloat16
F32 = jnp.float32


def halves(value):
    high = value.astype(BF16)
    low = (value - high.astype(F32)).astype(BF16)
    return high, low


def product(left, right, over=(1, 0)):
    dims = (((over[0],), (over[1],)), ((), ()))
    dot = functools.partial(lax.dot_general, dimension_numbers=dims, preferred_element_type=F32)
    count = left[0].shape[0]
    both = dot(jnp.concatenate(left, axis=0), right[0])
    return both[:count] + (both[count:] + dot(left[0], right[1]))


def shape(dims, dtype=F32):
    return jax.ShapeDtypeStruct(dims, dtype)


class Places:
    def __init__(self, terms, rows, slab):
        self.terms, self.rows, self.slab = terms, rows, slab
        self.cores = 2
        self.chips = terms // self.cores
        self.piece = slab // terms
        self.half = slab // self.cores

    def here(self):
        term = lax.axis_index("terms")
        return term // self.cores, term % self.cores, lax.axis_index("rows")

    def swap(self, value, chip=0, core=0, row=0):
        pairs = []
        for term in range(self.terms):
            for line in range(self.rows):
                other = term ^ (chip * self.cores + core)
                pairs.append((term * self.rows + line, other * self.rows + (line ^ row)))
        return lax.ppermute(value, ("terms", "rows"), pairs)


def order_left(places, left):
    width = left.shape[1]
    piece, half = places.piece, places.half

    def kernel(left_ref, own_ref, away_ref, lh_ref, ll_ref):
        chip, core, _ = places.here()
        for side, out in enumerate((own_ref, away_ref)):
            for slot in range(places.chips):
                source = pl.multiple_of((core ^ side) * half + (chip ^ slot) * piece, 8)
                out[pl.ds(slot * piece, piece), :] = left_ref[pl.ds(source, piece), :]
            rows = pl.ds(side * half, half)
            lh_ref[rows, :], ll_ref[rows, :] = halves(out[...])

    return pl.pallas_call(
        kernel,
        out_shape=(shape((half, width)),) * 2 + (shape(left.shape, BF16),) * 2,
        in_specs=[VMEM],
        out_specs=(VMEM,) * 4,
        compiler_params=pltpu.CompilerParams(vmem_limit_bytes=4 * MIB),
        name="order_left",
    )(left)


def split_right(places, right, amplitudes):
    def kernel(right_ref, amplitudes_ref, rh_ref, rl_ref, copy_ref, base_ref):
        rh_ref[...], rl_ref[...] = halves(right_ref[...])
        copy_ref[...] = amplitudes_ref[...]
        chip, core, _ = places.here()
        start = pl.multiple_of(core * places.half + chip * places.piece, 8)
        base_ref[...] = amplitudes_ref[pl.ds(start, places.piece), :]

    return pl.pallas_call(
        kernel,
        out_shape=(shape(right.shape, BF16),) * 2
        + (shape(amplitudes.shape), shape((places.piece, right.shape[1]))),
        in_specs=[VMEM] * 2,
        out_specs=(VMEM,) * 4,
        compiler_params=pltpu.CompilerParams(vmem_limit_bytes=4 * MIB),
        name="split_right",
    )(right, amplitudes)


def pair_pieces(places, own, received):
    piece = places.piece
    width = own.shape[1]

    def kernel(own_ref, received_ref, *outs):
        for slot, out in enumerate(outs):
            rows = pl.ds(slot * piece, piece)
            out[pl.ds(0, piece), :] = own_ref[rows, :]
            out[pl.ds(piece, piece), :] = received_ref[rows, :]

    return pl.pallas_call(
        kernel,
        out_shape=(shape((2 * piece, width)),) * places.chips,
        in_specs=[VMEM, VMEM],
        out_specs=(VMEM,) * places.chips,
        compiler_params=pltpu.CompilerParams(vmem_limit_bytes=2 * MIB),
        name="pair_pieces",
    )(own, received)


def exchange(places, own, away):
    received = places.swap(away, core=1)
    first, *others = pair_pieces(places, own, received)
    return [first] + to_chips(places, others)


def to_chips(places, parts):
    swapped = [places.swap(part, chip=slot) for slot, part in reversed(list(enumerate(parts, 1)))]
    return swapped[::-1]


def by_source(places, parts, whole, stride):
    chip, core, _ = places.here()
    piece = places.piece
    for slot, part in enumerate(parts):
        for side in range(places.cores):
            start = pl.multiple_of((chip ^ slot) * stride[0] + (core ^ side) * stride[1], 8)
            whole[pl.ds(start, piece), :] = part[pl.ds(side * piece, piece), :]


def combine_exchanged(places, parts, source_list, list_count, weight_index, weight_table):
    fan = source_list.shape[1]
    source_list, weight_index = source_list.T, weight_index.T
    width = parts[0].shape[1]
    piece, half = places.piece, places.half

    def kernel(source_ref, count_ref, index_ref, table_ref, *refs):
        *ins, own_ref, away_ref, whole = refs
        by_source(places, ins, whole, (places.cores * piece, piece))
        chip, core, _ = places.here()
        for side, out in enumerate((own_ref, away_ref)):
            for slot in range(places.chips):
                j = (chip ^ slot) * places.cores + (core ^ side)
                total = None
                for c in range(fan):
                    weight = jnp.where(c < count_ref[j], table_ref[index_ref[c, j]], 0.0)
                    start = pl.multiple_of(source_ref[c, j] * piece, 8)
                    term = weight * whole[pl.ds(start, piece), :]
                    total = term if total is None else total + term
                out[pl.ds(slot * piece, piece), :] = total

    return pl.pallas_call(
        kernel,
        out_shape=(shape((half, width)),) * 2,
        in_specs=[SMEM] * 4 + [VMEM] * len(parts),
        out_specs=(VMEM, VMEM),
        scratch_shapes=[pltpu.VMEM((places.slab, width), F32)],
        compiler_params=pltpu.CompilerParams(vmem_limit_bytes=4 * MIB),
        name="combine",
    )(source_list, list_count, weight_index, weight_table, *parts)


def place_rows(places, parts):
    width = parts[0].shape[1]

    def kernel(*refs):
        by_source(places, refs[:-1], refs[-1], (places.piece, places.half))

    return pl.pallas_call(
        kernel,
        out_shape=shape((places.slab, width)),
        in_specs=[VMEM] * len(parts),
        out_specs=VMEM,
        compiler_params=pltpu.CompilerParams(vmem_limit_bytes=2 * MIB),
        name="place_rows",
    )(*parts)


def assemble(places, layout, parts, store):
    chip, core, line = places.here()
    for (core_slot, blocks), part in zip(layout, parts):
        first = 0
        for row_slot, height, place in blocks:
            start = (line ^ row_slot) * places.slab + place(chip, core ^ core_slot)
            store(pl.multiple_of(start, 8), height, part[pl.ds(first, height), :])
            first += height


def put_in(whole):
    def store(start, height, value):
        whole[pl.ds(start, height), :] = value

    return store


def apply_terms(places, layout, parts, prepared):
    width = parts[0].shape[1]
    half = places.half
    *left_halves, rh, rl = prepared

    def first_kernel(*refs):
        count = len(parts)
        lh_ref, ll_ref, rh_ref, rl_ref, send_ref, mh_ref, ml_ref, whole = refs[count:]
        assemble(places, layout, refs[:count], put_in(whole))
        mapped = product((lh_ref[...], ll_ref[...]), halves(whole[...]))
        high, low = halves(mapped)
        send_ref[...] = product((high[half:], low[half:]), (rh_ref[...], rl_ref[...]))
        mh_ref[...], ml_ref[...] = high[:half], low[:half]

    def second_kernel(mh_ref, ml_ref, rh_ref, rl_ref, keep_ref):
        keep_ref[...] = product((mh_ref[...], ml_ref[...]), (rh_ref[...], rl_ref[...]))

    send, high, low = pl.pallas_call(
        first_kernel,
        out_shape=(shape((half, width)),) + (shape((half, width), BF16),) * 2,
        in_specs=[VMEM] * (len(parts) + 4),
        out_specs=(VMEM,) * 3,
        scratch_shapes=[pltpu.VMEM((width, width), F32)],
        compiler_params=pltpu.CompilerParams(vmem_limit_bytes=10 * MIB),
        name="apply",
    )(*parts, *left_halves, rh, rl)
    received = places.swap(send, core=1)
    keep = pl.pallas_call(
        second_kernel,
        out_shape=shape((half, width)),
        in_specs=[VMEM] * 4,
        out_specs=VMEM,
        compiler_params=pltpu.CompilerParams(vmem_limit_bytes=4 * MIB),
        name="apply_rest",
    )(high, low, rh, rl)
    return keep, received


def add_pieces(places, keep, received):
    piece = places.piece
    width = keep.shape[1]

    def kernel(keep_ref, received_ref, *outs):
        for slot, out in enumerate(outs):
            rows = pl.ds(slot * piece, piece)
            out[...] = keep_ref[rows, :] + received_ref[rows, :]

    return pl.pallas_call(
        kernel,
        out_shape=(shape((piece, width)),) * places.chips,
        in_specs=[VMEM, VMEM],
        out_specs=(VMEM,) * places.chips,
        compiler_params=pltpu.CompilerParams(vmem_limit_bytes=2 * MIB),
        name="add_pieces",
    )(keep, received)


def step_piece(base, pieces, copies):
    def kernel(base_ref, *refs):
        ins, outs = refs[: len(pieces)], refs[len(pieces) :]
        total = ins[0][...]
        for ref in ins[1:]:
            total = total + ref[...]
        for out in outs:
            out[...] = base_ref[...] - STEP * total

    return pl.pallas_call(
        kernel,
        out_shape=(shape(base.shape),) * copies,
        in_specs=[VMEM] * (1 + len(pieces)),
        out_specs=(VMEM,) * copies,
        compiler_params=pltpu.CompilerParams(vmem_limit_bytes=2 * MIB),
        name="step_piece",
    )(base, *pieces)


def stack(parts):
    width = parts[0].shape[1]
    heights = [part.shape[0] for part in parts]

    def kernel(*refs):
        out = refs[-1]
        start = 0
        for ref, height in zip(refs[:-1], heights):
            out[pl.ds(start, height), :] = ref[...]
            start += height

    return pl.pallas_call(
        kernel,
        out_shape=shape((sum(heights), width)),
        in_specs=[VMEM] * len(parts),
        out_specs=VMEM,
        compiler_params=pltpu.CompilerParams(vmem_limit_bytes=2 * MIB),
        name="stack",
    )(*parts)


def to_both_cores(places, layout, parts, blocks, part):
    other = places.swap(part, core=1)
    layout.extend([(0, blocks), (1, blocks)])
    parts.extend([part, other])


def spread(places, piece):
    slots = list(reversed(range(1, places.rows)))
    layout, parts = [], []

    def blocks(pairs):
        def place(slot):
            return lambda chip, core: core * places.half + (chip ^ slot) * places.piece

        return [(row_slot, places.piece, place(chip_slot)) for chip_slot, row_slot in pairs]

    lines = [places.swap(piece, row=slot) for slot in slots]
    own = [piece] + to_chips(places, [piece] * (places.chips - 1))
    mine = stack(lines)
    gathered = [mine] + to_chips(places, [mine] * (places.chips - 1))
    own = stack(own)
    to_both_cores(places, layout, parts, blocks([(slot, 0) for slot in range(places.chips)]), own)
    for chip_slot, part in enumerate(gathered):
        to_both_cores(places, layout, parts, blocks([(chip_slot, slot) for slot in slots]), part)
    return layout, parts


def spread_slabs(places, slab, ready):
    part_rows, piece = 2 * places.piece, places.piece
    slots = list(reversed(range(1, places.rows)))
    chip, core, _ = places.here()

    def parity(chip):
        return (chip & 1) ^ (chip >> 1)

    def place(turn, extra):
        return lambda chip, core: core * places.half + (parity(chip) ^ turn) * part_rows + extra

    start = core * places.half + parity(chip) * part_rows
    sent = lax.dynamic_slice_in_dim(slab, start, part_rows, 0)
    lines = [places.swap(sent, row=slot) for slot in slots]
    firsts, rests = stack_halves(lines)
    firsts, rests, *ready = lax.optimization_barrier((firsts, rests, *ready))
    layout, parts = [], []
    others = [places.swap(firsts, chip=1), places.swap(rests, chip=2)]
    for turn, extra, part in ((0, 0, firsts), (0, piece, rests), (1, 0, others[0]), (1, piece, others[1])):
        blocks = [(slot, piece, place(turn, extra)) for slot in slots]
        to_both_cores(places, layout, parts, blocks, part)
    return layout, parts, ready


def stack_halves(parts):
    width = parts[0].shape[1]
    height = parts[0].shape[0] // 2

    def kernel(*refs):
        for side, out in enumerate(refs[-2:]):
            for index, ref in enumerate(refs[:-2]):
                out[pl.ds(index * height, height), :] = ref[pl.ds(side * height, height), :]

    return pl.pallas_call(
        kernel,
        out_shape=(shape((height * len(parts), width)),) * 2,
        in_specs=[VMEM] * len(parts),
        out_specs=(VMEM,) * 2,
        compiler_params=pltpu.CompilerParams(vmem_limit_bytes=2 * MIB),
        name="stack_halves",
    )(*parts)


def reduced(places, keep, received):
    own, *others = add_pieces(places, keep, received)
    return [own] + to_chips(places, others)


def orthogonal(places, layout, parts):
    width = parts[0].shape[1]
    slab = places.slab
    tile = 256 if width % 256 == 0 else width
    blocks = width // tile

    def kernel(*refs):
        count = len(parts)
        slab_ref, high, low, mine_high, mine_low = refs[count : count + 5]
        iterate, gram, gram_high, gram_low, poly_high, poly_low, *spare = refs[count + 5 :]
        pairs = (spare[:2], spare[2:])
        assemble(places, layout, refs[:count], put_in(gram))
        squares = jnp.zeros((8, width), F32)
        for i in range(width // 8):
            some = gram[pl.ds(8 * i, 8), :]
            squares = squares + some * some
        values = gram[...].T * (1.0 / jnp.sqrt(jnp.sum(squares)))
        iterate[...] = values
        spare[0][...], spare[1][...] = halves(values)

        def symmetric(left, over, finish, out_high, out_low):
            for i in range(blocks):
                rows = pl.ds(i * tile, tile)
                rest = pl.ds(i * tile, width - i * tile)
                if over == (1, 1):
                    right = (left[0][rest, :], left[1][rest, :])
                else:
                    right = (left[0][:, rest], left[1][:, rest])
                strip = finish(product((left[0][rows, :], left[1][rows, :]), right, over), rows, rest)
                out_high[rows, rest], out_low[rows, rest] = halves(strip)
                for j in range(i + 1, blocks):
                    below = pl.ds(j * tile, tile)
                    mirrored = strip[:, (j - i) * tile : (j - i + 1) * tile].T
                    out_high[below, rows], out_low[below, rows] = halves(mirrored)

        def keep_gram(value, rows, rest):
            gram[rows, rest] = value
            return value

        def polynomial(value, rows, rest):
            return COEF_TWO * gram[rows, rest] + COEF_THREE * value

        for repeat in range(SWEEPS):
            here, there = pairs[repeat % 2], pairs[(repeat + 1) % 2]
            symmetric(here, (1, 1), keep_gram, gram_high, gram_low)
            symmetric((gram_high, gram_low), (1, 0), polynomial, poly_high, poly_low)
            for i in range(blocks):
                rows = pl.ds(i * tile, tile)
                moved = product((poly_high[rows, :], poly_low[rows, :]), (here[0][...], here[1][...]))
                values = COEF_ONE * iterate[rows, :] + moved
                if repeat < SWEEPS - 1:
                    iterate[rows, :] = values
                    there[0][rows, :], there[1][rows, :] = halves(values)
                else:
                    values = math.sqrt(width) * values
                    iterate[rows, :] = values
                    upright = values.T
                    gram[:, rows] = upright
                    high[:, rows], low[:, rows] = halves(upright)
        mine = pl.ds(pl.multiple_of(lax.axis_index("rows") * slab, 8), slab)
        slab_ref[...] = gram[mine, :]
        mine_high[...], mine_low[...] = halves(iterate[mine, :])

    square = (width, width)
    return pl.pallas_call(
        kernel,
        out_shape=(shape((slab, width)),) + (shape(square, BF16),) * 2 + (shape((slab, width), BF16),) * 2,
        in_specs=[VMEM] * len(parts),
        out_specs=(VMEM,) * 5,
        scratch_shapes=[pltpu.VMEM(square, F32)] * 2 + [pltpu.VMEM(square, BF16)] * 8,
        compiler_params=pltpu.CompilerParams(vmem_limit_bytes=24 * MIB),
        name="orthogonal",
    )(*parts)


def environment(places, layout, parts, isometry, high, low, mine_high, mine_low):
    width = high.shape[0]
    slab = places.slab

    def kernel(*refs):
        count = len(parts)
        iso_ref, high_ref, low_ref, mh_ref, ml_ref, iso_out, out_ref, block_high, block_low, sem = refs[count:]
        out = pltpu.make_async_copy(iso_ref, iso_out, sem)
        out.start()

        def store(start, height, value):
            block_high[pl.ds(start, height), :], block_low[pl.ds(start, height), :] = halves(value)

        assemble(places, layout, refs[:count], store)
        rotated = product((mh_ref[...], ml_ref[...]), (block_high[...], block_low[...]))
        out_ref[...] = product(halves(rotated), (high_ref[...], low_ref[...]))
        out.wait()

    return pl.pallas_call(
        kernel,
        out_shape=(shape((slab, width)),) * 2,
        in_specs=[VMEM] * (len(parts) + 5),
        out_specs=(pl.BlockSpec(memory_space=pl.ANY), VMEM),
        scratch_shapes=[pltpu.VMEM((width, width), BF16)] * 2 + [pltpu.SemaphoreType.DMA],
        compiler_params=pltpu.CompilerParams(vmem_limit_bytes=10 * MIB),
        name="environment",
    )(*parts, isometry, high, low, mine_high, mine_low)


def combine_pieces(pieces, source_list, list_count, weight_index, weight_table):
    fan = source_list.shape[1]

    def kernel(source_ref, count_ref, index_ref, table_ref, pieces_ref, out_ref):
        for j in range(source_list.shape[0]):
            total = None
            for c in range(fan):
                weight = jnp.where(c < count_ref[j], table_ref[index_ref[j, c]], 0.0)
                term = weight * pieces_ref[source_ref[j, c]]
                total = term if total is None else total + term
            out_ref[j] = total

    return pl.pallas_call(
        kernel,
        out_shape=shape((source_list.shape[0],) + pieces.shape[1:]),
        in_specs=[SMEM] * 4 + [VMEM],
        out_specs=VMEM,
        compiler_params=pltpu.CompilerParams(vmem_limit_bytes=4 * MIB),
        name="combine",
    )(source_list, list_count, weight_index, weight_table, pieces)


def combined_slab(left, source_list, list_count, weight_index, weight_table):
    rows, width = left.shape
    owners = lax.axis_size("terms")
    if rows % (8 * owners) == 0:
        run = (rows // owners, width)
    else:
        run = (1, rows * width // owners)
    pieces = lax.all_to_all(left.reshape((owners,) + run), "terms", 0, 0, tiled=True)
    mixed = combine_pieces(pieces, source_list, list_count, weight_index, weight_table)
    return lax.all_to_all(mixed, "terms", 0, 0, tiled=True).reshape(rows, width)


def body(amplitudes, left_terms, right_terms, source_list, list_count, weight_index, weight_table):
    left, right = left_terms[0], right_terms[0]
    slab, _ = left.shape
    terms, rows = lax.axis_size("terms"), lax.axis_size("rows")
    places = Places(terms, rows, slab)

    lists = (source_list, list_count, weight_index, weight_table)
    _, _, line = places.here()
    every = list(range(rows))
    slabs = [(0, [(slot, slab, lambda chip, core: 0)]) for slot in every]
    if swappable(terms, rows, slab):
        own, away, *left_halves = order_left(places, left)
        prepared = (*left_halves, *split_right(places, right, amplitudes))
        pieces = exchange(places, own, away)
        own, away = combine_exchanged(places, pieces, *lists)
        combined = place_rows(places, exchange(places, own, away))
        layout, parts, prepared = spread_slabs(places, amplitudes, prepared)
        *prepared, amplitudes, base = prepared
        layout, parts = [slabs[0]] + layout, [amplitudes] + parts
        for name in ("f", "x"):
            pieces = reduced(places, *apply_terms(places, layout, parts, prepared))
            sent, *kept = step_piece(base, pieces, 2 if name == "f" else 1)
            layout, parts = spread(places, sent)
            base = kept[0] if kept else None
        blocks = [combined]
        for slot in every[1:]:
            blocks.append(places.swap(combined, row=slot))
    else:
        matrix = amplitudes
        for _ in range(2):
            full = lax.all_gather(matrix, "rows", axis=0, tiled=True)
            mapped = jnp.dot(left, full, precision=HIGH)
            summed = lax.psum(jnp.dot(mapped, right, precision=HIGH), "terms")
            matrix = matrix - STEP * summed
        full = lax.all_gather(matrix, "rows", axis=0, tiled=True)
        layout = slabs
        parts = [lax.dynamic_slice_in_dim(full, (line ^ slot) * slab, slab, 0) for slot in every]
        combined = combined_slab(left, *lists)
        full = lax.all_gather(combined, "rows", axis=0, tiled=True)
        blocks = [lax.dynamic_slice_in_dim(full, (line ^ slot) * slab, slab, 0) for slot in every]
    isometry, new_environment = environment(places, slabs, blocks, *orthogonal(places, layout, parts))
    return (isometry, new_environment[None])


def swappable(terms, rows, slab):
    return terms == 8 and rows & (rows - 1) == 0 and slab % (8 * terms) == 0


def solution(mesh):
    placed = (P("rows", None), P("terms", "rows", None), P("terms", None, None), P(), P(), P(), P())

    return jax.shard_map(
        body,
        mesh=mesh,
        in_specs=placed,
        out_specs=(P("rows", None), P("terms", "rows", None)),
        check_vma=False,
    )
```
